512 devices in a mesh: gx: 16 (over y, core), gy: 32 (over z, x).
Axes of the slice: x: 4, y: 8, z: 8, core: 2. Of those that a mesh axis runs over, the one named last changes fastest.
Arguments:
- query_rows: bfloat16 [65536, 1024], P(('gx', 'gy')), may hold values from -6 to 6
- key_rows: bfloat16 [65536, 1024], P(('gx', 'gy')), may hold values from -6 to 6
- value_rows: bfloat16 [65536, 1024], P(('gx', 'gy')), may hold values from -6 to 6
- out_grad: bfloat16 [65536, 1024], P(('gx', 'gy')), may hold values from -6 to 6
- gate_class: int32 [65536], P(('gx', 'gy')), may hold values from 0 to 31
- gate_table: float32 [32, 20, 8], replicated, may hold values from 0 to 1, as said below
Outputs:
- query_grad: bfloat16 [65536, 1024], P(('gx', 'gy'))
- key_grad: bfloat16 [65536, 1024], P(('gx', 'gy'))
- value_grad: bfloat16 [65536, 1024], P(('gx', 'gy'))
The draws below stay inside these ranges and needn't reach their ends.
Inputs may be any that keep to these rules, and one draw needn't show every extreme that they name: `gate_class`: row of the gate table for each token. `gate_table`: every entry is positive.
All inputs are finite; a program needn't handle non-finite values.
Results may differ from the reference program's by a relative error of at most 0.0054.
Values may be sent and summed in bfloat16 or wider, within the bound.
A program may use at most 64 MiB of HBM per device.

```python
import jax
import jax.numpy as jnp
from jax import lax

TOK_DEV = 128
H = 8
HS = 128
G = 32
LEVELS = 20
TOKENS = 65536
HD = 1024


def draw_gate_table(key, part):
    level_index = jnp.arange(LEVELS, dtype=jnp.float32)
    spans = jnp.maximum(level_index - 1.0, 0.0)
    level_scale = jnp.exp2(-0.5 * spans) / jnp.sqrt(jnp.float32(HS))
    base = jnp.exp(jax.random.uniform(key, (G, LEVELS, H), jnp.float32, jnp.log(0.1), 0.0))
    return (base * level_scale[None, :, None]).astype(jnp.float32)


def touch_ends(drawn, key, smallest, high):
    dims = drawn.shape
    index_at = [jax.random.randint(jax.random.fold_in(key, axis), (), 0, dims[axis]) for axis in range(len(dims))]
    drawn = drawn.at[tuple(index_at)].set(smallest)
    longest = dims.index(max(dims))
    index_at[longest] = (index_at[longest] + 1) % dims[longest]
    return drawn.at[tuple(index_at)].set(high)


def block_levels(stream_key, shape, cuts, low, top_value):
    gain = 1.0
    for dim, blocks in cuts:
        heights = jax.random.uniform(jax.random.fold_in(jax.random.fold_in(stream_key, 6), dim), (blocks,), jnp.float32, low / len(cuts), top_value / len(cuts))
        gain = gain * jnp.repeat(jnp.exp(heights), shape[dim] // blocks).reshape((-1,) + (1,) * (len(shape) - 1 - dim))
    return gain


def centred(rng, shape, spread, limit, cuts=(), kind=jnp.bfloat16):
    values = spread * jax.random.normal(rng, shape, jnp.float32)
    if cuts:
        values = values * block_levels(rng, shape, cuts, -0.22, 0.18)
    return jnp.clip(values, -limit, limit).astype(kind)


def setup_inputs(seed: int = 0) -> dict:
    streams_of = jax.random.split(jax.random.key(seed), 7)
    query_rows = centred(streams_of[0], (TOKENS, HD), 1.0, 6.0, ((0, 512),))
    key_rows = centred(streams_of[1], (TOKENS, HD), 1.0, 6.0, ((0, 512),))
    value_rows = centred(streams_of[2], (TOKENS, HD), 1.0, 6.0, ((0, 512),))
    out_grad = centred(streams_of[3], (TOKENS, HD), 1.0, 6.0, ((0, 512),))
    gate_class = touch_ends(jax.random.randint(streams_of[4], (TOKENS,), 0, G), jax.random.fold_in(streams_of[4], 1), 0, G - 1).astype(jnp.int32)
    gate_table = draw_gate_table(jax.random.fold_in(streams_of[6], 71), 0)
    return {"query_rows": query_rows, "key_rows": key_rows, "value_rows": value_rows, "out_grad": out_grad, "gate_class": gate_class, "gate_table": gate_table}


def block_weights(gate_rows, amount):
    block_depth = amount.bit_length() - 1
    positions = jnp.arange(amount, dtype=jnp.int32)
    xor_place = jnp.bitwise_xor(positions[:, None], positions[None, :])
    level_map = jnp.zeros((amount, amount), jnp.int32)
    for bit_index in range(block_depth):
        level_map = level_map + (xor_place >= 2 ** bit_index).astype(jnp.int32)
    causal = positions[None, :] <= positions[:, None]
    weights = jnp.zeros((gate_rows.shape[2], amount, amount), jnp.float32)
    for tree_level in range(block_depth + 1):
        chosen = jnp.logical_and(level_map == tree_level, causal)
        picked = gate_rows[:, tree_level, :].T[:, :, None]
        weights = weights + jnp.where(chosen[None, :, :], picked, jnp.zeros((), weights.dtype))
    return weights


def to_bfloat(values):
    return lax.optimization_barrier(values.astype(jnp.bfloat16)).astype(jnp.float32)


def sibling_sums(values, span):
    number = values.shape[0]
    rest = values.shape[1:]
    blocks = jnp.sum(values.reshape((number // span, span) + rest), axis=1)
    pairs = blocks.reshape((number // (2 * span), 2) + rest)[:, ::-1]
    flipped = pairs.reshape((number // span,) + rest)
    return jnp.repeat(flipped, span, axis=0)


def reference(query_rows, key_rows, value_rows, out_grad, gate_class, gate_table):
    group_count = TOKENS // TOK_DEV
    block_depth = TOK_DEV.bit_length() - 1
    device_depth = group_count.bit_length() - 1
    gates = gate_table[gate_class].astype(jnp.float32)
    gate_blocks = gates.reshape(group_count, TOK_DEV, LEVELS, H)
    shape_four = (group_count, TOK_DEV, H, HS)
    query_f = query_rows.reshape(shape_four).astype(jnp.float32)
    key_f = key_rows.reshape(shape_four).astype(jnp.float32)
    value_f = value_rows.reshape(shape_four).astype(jnp.float32)
    grad_f = out_grad.reshape(shape_four).astype(jnp.float32)

    def local_block(pieces):
        query_part, key_part, value_part, grad_part, gate_part = pieces
        scores = jnp.einsum('thd,shd->hts', query_part, key_part)
        pair_grads = jnp.einsum('the,she->hts', grad_part, value_part)
        weights = block_weights(gate_part, TOK_DEV)
        weighted_grads = to_bfloat(weights * pair_grads)
        weighted_scores = to_bfloat(weights * scores)
        local_query = jnp.einsum('hts,shd->thd', weighted_grads, key_part)
        local_key = jnp.einsum('hts,thd->shd', weighted_grads, query_part)
        local_value = jnp.einsum('hts,the->she', weighted_scores, grad_part)
        return local_query, local_key, local_value

    local_query, local_key, local_value = lax.map(local_block, (query_f, key_f, value_f, grad_f, gate_blocks))
    group_states = jnp.einsum('nthd,nthe->nhde', key_f, value_f)
    group_ids = jnp.arange(group_count, dtype=jnp.int32)
    query_grad = local_query
    state_grad = jnp.zeros_like(group_states)
    for tree_level in range(device_depth):
        span = 2 ** tree_level
        flags = ((group_ids // span) % 2).astype(jnp.float32)
        gate_level = gate_blocks[:, :, block_depth + 1 + tree_level, :] * flags[:, None, None]
        rounded_state = to_bfloat(sibling_sums(group_states, span))
        query_grad = query_grad + gate_level[..., None] * jnp.einsum('nthe,nhde->nthd', grad_f, rounded_state)
        scaled_query = to_bfloat(gate_level[..., None] * query_f)
        level_grad = jnp.einsum('nthd,nthe->nhde', scaled_query, grad_f)
        state_grad = state_grad + sibling_sums(level_grad, span)
    rounded_grad = to_bfloat(state_grad)
    key_grad = local_key + jnp.einsum('nthe,nhde->nthd', value_f, rounded_grad)
    value_grad = local_value + jnp.einsum('nthd,nhde->nthe', key_f, rounded_grad)
    return (query_grad.reshape(TOKENS, H * HS).astype(jnp.bfloat16),
            key_grad.reshape(TOKENS, H * HS).astype(jnp.bfloat16),
            value_grad.reshape(TOKENS, H * HS).astype(jnp.bfloat16))
```

```python
import jax
import jax.numpy as jnp
from jax import lax
from jax.experimental import pallas as pl
from jax.experimental.pallas import tpu as pltpu
from jax.sharding import PartitionSpec as P

MESH = pl.DeviceIdType.MESH
F32 = jnp.float32
BF16 = jnp.bfloat16
N = 128
HEADS = 8
KQ, KG, KT, KS, KU, KB, KV, KW, KC, KD = range(10)


def mm(a, b, ca, cb):
    return lax.dot_general(a, b, (((ca,), (cb,)), ((), ())), preferred_element_type=F32)


def nn(a, b):
    return mm(a, b, 1, 0)


def nt(a, b):
    return mm(a, b, 1, 1)


def tn(a, b):
    return mm(a, b, 0, 0)


def kernel(
    q_ref, k_ref, v_ref, g_ref, cls_ref, tab_ref,
    qo_ref, ko_ref, vo_ref,
    gates, lev_ref, st_send, qb, gb, sb, gtb, sq, qloc, kloc, vloc,
    lbuf, urecv, bsend, brecv, vsend, rbuf, ctr, dacc, csend, dsend, crecv, drecv,
    ssem, rsem,
):
    gx = lax.axis_index("gx")
    gy = lax.axis_index("gy")
    y = gx // 2
    core = gx % 2
    zz = gy // 8
    p = gy % 8
    a = core * 4 + zz

    def dev_p(r):
        return (gx, zz * 8 + r)

    def dev_a(r):
        return (y * 2 + r // 4, (r % 4) * 8 + p)

    def dev_y(r):
        return (r * 2 + core, gy)

    barrier = pltpu.get_barrier_semaphore()
    for i in range(1, 8):
        for dev in (dev_p((p + i) % 8), dev_a((a + i) % 8), dev_y((y + i) % 8)):
            pl.semaphore_signal(barrier, inc=1, device_id=dev, device_id_type=MESH)

    sends = []

    def send(kind, r, src, dst, slot, dev):
        copy = pltpu.make_async_remote_copy(
            src_ref=src, dst_ref=dst, send_sem=ssem.at[kind, r], recv_sem=rsem.at[kind, slot],
            device_id=dev, device_id_type=MESH,
        )
        copy.start()
        sends.append(copy)

    def local(kind, src, dst, slot):
        pltpu.make_async_copy(src, dst, rsem.at[kind, slot]).start()

    def arrived(kind, dst, slot):
        pltpu.make_async_copy(dst, dst, rsem.at[kind, slot]).wait()

    def cols(ref, r):
        return ref.at[:, pl.ds(pl.multiple_of(r * N, N), N)]

    classes = lax.broadcasted_iota(jnp.int32, (32, N), 0)
    onehot = (classes == cls_ref[...]).astype(F32)
    gates[...] = lax.dot_general(
        tab_ref[...], onehot, (((1,), (0,)), ((), ())),
        precision=lax.Precision.HIGHEST, preferred_element_type=F32,
    )
    brecv[y] = jnp.zeros((16, N), F32)

    pl.semaphore_wait(barrier, 21)

    for i in range(1, 8):
        r = (p + i) % 8
        send(KQ, i, cols(q_ref, r), qb.at[p], p, dev_p(r))
        send(KG, i, cols(g_ref, r), gb.at[p], p, dev_p(r))
        send(KT, i, gates.at[pl.ds(pl.multiple_of(r * 24 + 8, 8), 16), :], gtb.at[p], p, dev_p(r))
    local(KQ, cols(q_ref, p), qb.at[p], p)
    local(KG, cols(g_ref, p), gb.at[p], p)
    local(KT, gates.at[pl.ds(pl.multiple_of(p * 24 + 8, 8), 16), :], gtb.at[p], p)

    for h in range(HEADS):
        c = slice(h * N, h * N + N)
        st_send[h] = tn(k_ref[:, c], v_ref[:, c]).astype(BF16)
    for i in range(1, 8):
        r = (p + i) % 8
        send(KS, i, st_send.at[r], sb.at[p], p, dev_p(r))
    local(KS, st_send.at[p], sb.at[p], p)

    s_id = lax.broadcasted_iota(jnp.int32, (N, N), 0)
    t_id = lax.broadcasted_iota(jnp.int32, (N, N), 1)
    place = jnp.bitwise_xor(s_id, t_id)
    level = jnp.zeros((N, N), jnp.int32)
    for bit in range(7):
        level = level + (place >= 2**bit).astype(jnp.int32)
    lev_ref[...] = jnp.where(s_id <= t_id, level, -1)

    def own_head(h, _):
        c = pl.ds(pl.multiple_of(h * N, N), N)
        q = q_ref[:, c]
        k = k_ref[:, c]
        v = v_ref[:, c]
        g = g_ref[:, c]
        rows = gates[pl.ds(pl.multiple_of(h * 24, 8), 8), :]
        lev = lev_ref[...]
        w = jnp.zeros((N, N), F32)
        for l in range(8):
            w = jnp.where(lev == l, rows[l : l + 1, :], w)
        wg = (w * nt(v, g)).astype(BF16)
        ws = (w * nt(k, q)).astype(BF16)
        kloc[:, c] = nn(wg, q)
        vloc[:, c] = nn(ws, g)
        qloc[:, c] = tn(wg, k)
        return 0

    lax.fori_loop(0, HEADS, own_head, 0)

    low = {}
    for r in range(8):
        arrived(KQ, qb.at[r], r)
        arrived(KG, gb.at[r], r)
        arrived(KT, gtb.at[r], r)
        qt = qb[r].T.astype(F32)
        rows = gtb[r]
        for l in range(3, 9):
            sq[(l - 3) * N : (l - 2) * N, r * N : (r + 1) * N] = (qt * rows[l : l + 1, :]).astype(BF16)
        for l in range(3):
            if r >> l & 1:
                part = nn((qt * rows[l : l + 1, :]).astype(BF16), gb[r])
                key = (l, r >> l)
                low[key] = low[key] + part if key in low else part
    for b in range(8):
        acc = jnp.zeros((N, N), F32)
        for l in range(3):
            if not b >> l & 1:
                acc = acc + low[(l, (b >> l) ^ 1)]
        dacc[b] = acc
    grads = nn(sq[...], gb[...].reshape(8 * N, N))
    lbuf[1:7] = grads.astype(BF16).reshape(6, N, N)
    states = []
    for r in range(8):
        arrived(KS, sb.at[r], r)
        states.append(sb[r].astype(F32))
    pair = [states[2 * j] + states[2 * j + 1] for j in range(4)]
    quad = [pair[0] + pair[1], pair[2] + pair[3]]
    lbuf[0] = (quad[0] + quad[1]).astype(BF16)
    for i in range(1, 8):
        r = (a + i) % 8
        send(KU, i, lbuf.at[:, pl.ds(pl.multiple_of(r * 16, 16), 16), :], urecv.at[a], a, dev_a(r))
    local(KU, lbuf.at[:, pl.ds(pl.multiple_of(a * 16, 16), 16), :], urecv.at[a], a)

    for b in range(8):
        acc = jnp.zeros((N, N), F32)
        rows = gtb[b]
        for l in range(3):
            if b >> l & 1:
                other = (b >> l) ^ 1
                left = sb[other] if l == 0 else (pair, quad)[l - 1][other].astype(BF16)
                acc = acc + rows[l : l + 1, :] * nt(left, gb[b])
        ctr[b] = acc

    tops = []
    lows = {l: [] for l in range(3, 9)}
    for r in range(8):
        arrived(KU, urecv.at[r], r)
        tops.append(urecv[r, 0].astype(F32))
        for l in range(3, 9):
            lows[l].append(urecv[r, l - 2].astype(F32))
    tpair = [tops[2 * j] + tops[2 * j + 1] for j in range(4)]
    tquad = [tpair[0] + tpair[1], tpair[2] + tpair[3]]
    bsend[0] = tquad[0] + tquad[1]
    for l in range(6, 9):
        total = lows[l][0]
        for r in range(1, 8):
            total = total + lows[l][r]
        bsend[l - 5] = total
    for i in range(1, 8):
        r = (y + i) % 8
        high = jnp.where(y // 4 != r // 4, 3, jnp.where(y // 2 != r // 2, 2, 1))
        pick = jnp.where(y < r, 0, high)
        send(KB, i, bsend.at[pick], brecv.at[y], y, dev_y(r))
    zero = jnp.zeros((16, N), F32)
    l4 = {3: lows[4][2] + lows[4][3], 7: lows[4][6] + lows[4][7]}
    l5 = (lows[5][4] + lows[5][5]) + (lows[5][6] + lows[5][7])
    dmid = []
    for r in range(8):
        vsend[r, 0] = (tops[r - 1] if r & 1 else zero).astype(BF16)
        vsend[r, 1] = (tpair[(r >> 1) ^ 1] if r & 2 else zero).astype(BF16)
        vsend[r, 2] = (tquad[0] if r & 4 else zero).astype(BF16)
        acc = zero
        if not r & 1:
            acc = acc + lows[3][r + 1]
        if not r & 2:
            acc = acc + l4[r | 3]
        if not r & 4:
            acc = acc + l5
        dmid.append(acc)
    mine = pl.ds(pl.multiple_of(a * 16, 16), 16)
    for i in range(1, 8):
        r = (a + i) % 8
        send(KV, i, vsend.at[r, pl.ds(0, 3)], rbuf.at[pl.ds(0, 3), mine, :], a, dev_a(r))
    local(KV, vsend.at[a, pl.ds(0, 3)], rbuf.at[pl.ds(0, 3), mine, :], a)

    for r in range(8):
        arrived(KV, rbuf.at[pl.ds(0, 3), pl.ds(16 * r, 16), :], r)

    def middle(b, _):
        rows = gtb[b]
        prod = nt(rbuf[0:3].reshape(3 * N, N), gb[b])
        acc = ctr[b]
        for l in range(3):
            acc = acc + rows[3 + l : 4 + l, :] * prod[l * N : (l + 1) * N]
        ctr[b] = acc
        return 0

    lax.fori_loop(0, 8, middle, 0, unroll=2)

    for i in range(1, 8):
        arrived(KB, brecv.at[(y + i) % 8], (y + i) % 8)
    s6, s7, s8, dtop = zero, zero, zero, zero
    for r in range(8):
        got = brecv[r]
        before = r < y
        s6 = s6 + jnp.where(jnp.logical_and(before, r // 2 == y // 2), got, 0.0)
        s7 = s7 + jnp.where(
            jnp.logical_and(before, jnp.logical_and(r // 4 == y // 4, r // 2 != y // 2)), got, 0.0
        )
        s8 = s8 + jnp.where(jnp.logical_and(before, r // 4 != y // 4), got, 0.0)
        dtop = dtop + jnp.where(r > y, got, 0.0)
    for r in range(8):
        vsend[r, 3] = s6.astype(BF16)
        vsend[r, 4] = s7.astype(BF16)
        vsend[r, 5] = s8.astype(BF16)
        vsend[r, 6] = (dmid[r] + dtop).astype(BF16)
    for i in range(1, 8):
        r = (a + i) % 8
        send(KW, i, vsend.at[r, pl.ds(3, 4)], rbuf.at[pl.ds(3, 4), mine, :], a, dev_a(r))
    local(KW, vsend.at[a, pl.ds(3, 4)], rbuf.at[pl.ds(3, 4), mine, :], a)
    for r in range(8):
        arrived(KW, rbuf.at[pl.ds(3, 4), pl.ds(16 * r, 16), :], r)

    for b in range(8):
        dsend[b] = (dacc[b] + rbuf[6].astype(F32)).astype(BF16)
    for i in range(1, 8):
        r = (p + i) % 8
        send(KD, i, dsend.at[r], drecv.at[p], p, dev_p(r))
    local(KD, dsend.at[p], drecv.at[p], p)

    def upper(b, _):
        rows = gtb[b]
        prod = nt(rbuf[3:6].reshape(3 * N, N), gb[b])
        acc = ctr[b]
        for l in range(3):
            acc = acc + rows[6 + l : 7 + l, :] * prod[l * N : (l + 1) * N]
        csend[b] = acc.T.astype(BF16)
        return 0

    lax.fori_loop(0, 8, upper, 0, unroll=2)
    for i in range(1, 8):
        r = (p + i) % 8
        send(KC, i, csend.at[r], crecv.at[p], p, dev_p(r))
    local(KC, csend.at[p], crecv.at[p], p)

    for h in range(HEADS):
        c = slice(h * N, h * N + N)
        arrived(KD, drecv.at[h], h)
        d = drecv[h]
        ko_ref[:, c] = (kloc[:, c] + nt(v_ref[:, c], d)).astype(BF16)
        vo_ref[:, c] = (vloc[:, c] + nn(k_ref[:, c], d)).astype(BF16)
    for h in range(HEADS):
        c = slice(h * N, h * N + N)
        arrived(KC, crecv.at[h], h)
        qo_ref[:, c] = (qloc[:, c] + crecv[h].astype(F32)).astype(BF16)
    for copy in sends:
        copy.wait_send()


def per_device(query_rows, key_rows, value_rows, out_grad, gate_class, gate_table):
    table = jnp.pad(gate_table.transpose(2, 1, 0), ((0, 0), (0, 4), (0, 0))).reshape(24 * HEADS, 32)
    out = jax.ShapeDtypeStruct((N, HEADS * N), BF16)
    vmem = pl.BlockSpec(memory_space=pltpu.VMEM)
    cube = lambda n, dtype: pltpu.VMEM((n, N, N), dtype)
    wide = pltpu.VMEM((N, HEADS * N), F32)
    return pl.pallas_call(
        kernel,
        out_shape=(out, out, out),
        in_specs=[vmem] * 6,
        out_specs=(vmem, vmem, vmem),
        scratch_shapes=[
            pltpu.VMEM((24 * HEADS, N), F32),
            pltpu.VMEM((N, N), jnp.int32),
            cube(8, BF16), cube(8, BF16), cube(8, BF16), cube(8, BF16),
            pltpu.VMEM((8, 16, N), F32),
            pltpu.VMEM((6 * N, 8 * N), BF16),
            wide, wide, wide,
            cube(7, BF16),
            pltpu.VMEM((8, 7, 16, N), BF16),
            pltpu.VMEM((4, 16, N), F32),
            pltpu.VMEM((8, 16, N), F32),
            pltpu.VMEM((8, 7, 16, N), BF16),
            cube(7, BF16),
            cube(8, F32), cube(8, F32),
            cube(8, BF16), cube(8, BF16), cube(8, BF16), cube(8, BF16),
            pltpu.SemaphoreType.DMA((10, 8)),
            pltpu.SemaphoreType.DMA((10, 8)),
        ],
        compiler_params=pltpu.CompilerParams(
            collective_id=0, has_side_effects=True, vmem_limit_bytes=40 * 1024 * 1024
        ),
    )(query_rows, key_rows, value_rows, out_grad, gate_class.reshape(1, N), table)


def solution(mesh):
    rows = P(("gx", "gy"), None)
    return jax.shard_map(
        per_device,
        mesh=mesh,
        in_specs=(rows, rows, rows, rows, P(("gx", "gy")), P()),
        out_specs=(rows, rows, rows),
        check_vma=False,
    )
```

```python
import jax
import jax.numpy as jnp
from jax import lax
from jax.experimental import pallas as pl
from jax.experimental.pallas import tpu as pltpu
from jax.sharding import PartitionSpec as P

MESH = pl.DeviceIdType.MESH
F32 = jnp.float32
BF16 = jnp.bfloat16
N = 128
HEADS = 8
KQ, KG, KT, KS, KL, KU, KB, KV, KW, KX, KC, KD = 0, 1, 2, 3, 4, 10, 11, 12, 15, 16, 19, 20
KINDS = 21
NEAR = ((0, 1), (0, 3), (1, 0), (1, 1), (1, 3), (0, 2), (1, 2))
FAR = ((0, 2), (1, 2), (0, 1), (0, 3), (1, 1), (1, 3), (1, 0))


def mm(a, b, ca, cb):
    return lax.dot_general(a, b, (((ca,), (cb,)), ((), ())), preferred_element_type=F32)


def nn(a, b):
    return mm(a, b, 1, 0)


def nt(a, b):
    return mm(a, b, 1, 1)


def tn(a, b):
    return mm(a, b, 0, 0)


def kernel(
    q_hbm, k_hbm, v_hbm, g_hbm, cls_hbm, tab_hbm,
    qo_ref, ko_ref, vo_ref,
    q_ref, k_ref, v_ref, g_ref, cls_ref, tab_ref,
    gates, hg, lev_ref, st_send, qb, gb, sb, gtb, lacc, qloc, kloc, vloc,
    lbuf, urecv, bsend, brecv, ysum, vsend, wsend, xsend, rbuf, ctr, dacc, csend, dsend, crecv, drecv,
    lsem, ssem, rsem,
):
    gx = lax.axis_index("gx")
    gy = lax.axis_index("gy")
    y = gx // 2
    core = gx % 2
    zz = gy // 8
    p = gy % 8
    z0 = p // 4
    x = p % 4
    a = core * 4 + zz
    flag = {3: zz % 2, 4: zz // 2, 5: core, 6: y % 2, 7: y // 2 % 2, 8: y // 4}
    near = [(z0 + dz) % 2 * 4 + (x + dx) % 4 for dz, dx in NEAR]
    far = [(core + dc) % 2 * 4 + (zz + dz) % 4 for dc, dz in FAR]

    def dev_p(r):
        return (gx, zz * 8 + r)

    def dev_a(r):
        return (y * 2 + r // 4, (r % 4) * 8 + p)

    def dev_y(r):
        return (r * 2 + core, gy)

    barrier = pltpu.get_barrier_semaphore()
    for i in range(7):
        for dev in (dev_p(near[i]), dev_a(far[i]), dev_y((y + i + 1) % 8)):
            pl.semaphore_signal(barrier, inc=1, device_id=dev, device_id_type=MESH)

    loads = []
    for i, (src, dst) in enumerate((
        (cls_hbm, cls_ref), (tab_hbm, tab_ref), (q_hbm, q_ref), (g_hbm, g_ref), (k_hbm, k_ref), (v_hbm, v_ref),
    )):
        loads.append(pltpu.make_async_copy(src, dst, lsem.at[i]))
        loads[-1].start()

    sends = []

    def send(kind, i, src, dst, slot, dev, keep=sends):
        pltpu.make_async_remote_copy(
            src_ref=src, dst_ref=dst, send_sem=ssem.at[kind, i], recv_sem=rsem.at[kind, slot],
            device_id=dev, device_id_type=MESH,
        ).start()
        keep.append((kind, i))

    def sent(done):
        for kind, i in done:
            if kind < KL and kind != KT or kind >= KC:
                like = qb.at[0]
            elif kind == KT:
                like = gtb.at[0]
            elif kind == KB:
                like = brecv.at[0]
            else:
                like = urecv.at[0, 0]
            pltpu.make_async_copy(like, like, ssem.at[kind, i]).wait()

    def local(kind, src, dst, slot):
        pltpu.make_async_copy(src, dst, rsem.at[kind, slot]).start()

    def arrived(kind, dst, slot):
        pltpu.make_async_copy(dst, dst, rsem.at[kind, slot]).wait()

    def cols(ref, r):
        return ref.at[:, pl.ds(pl.multiple_of(r * N, N), N)]

    def rows16(r):
        return pl.ds(pl.multiple_of(r * 16, 16), 16)

    zero = jnp.zeros((16, N), F32)
    for l in range(3, 9):
        @pl.when(flag[l] == 0)
        def _():
            rbuf[l - 3] = jnp.zeros((N, N), BF16)
    loads[0].wait()
    loads[1].wait()
    classes = lax.broadcasted_iota(jnp.int32, (32, N), 0)
    onehot = (classes == cls_ref[...]).astype(F32)
    gates[...] = lax.dot_general(
        tab_ref[...].reshape(20 * HEADS, 32), onehot, (((1,), (0,)), ((), ())),
        precision=lax.Precision.HIGHEST, preferred_element_type=F32,
    )
    for h in range(HEADS):
        hg[h, 0:20] = gates[pl.ds(h, 20, stride=HEADS), :]
        hg[h, 20:24] = jnp.zeros((4, N), F32)
    loads[2].wait()
    loads[3].wait()

    pl.semaphore_wait(barrier, 21)

    for i, r in enumerate(near):
        send(KQ, i, cols(q_ref, r), qb.at[p], p, dev_p(r))
        send(KG, i, cols(g_ref, r), gb.at[p], p, dev_p(r))
        send(KT, i, hg.at[r, pl.ds(8, 16)], gtb.at[p], p, dev_p(r))
    local(KQ, cols(q_ref, p), qb.at[p], p)
    local(KG, cols(g_ref, p), gb.at[p], p)
    local(KT, hg.at[p, pl.ds(8, 16)], gtb.at[p], p)

    loads[4].wait()
    loads[5].wait()
    for h in range(HEADS):
        c = slice(h * N, h * N + N)
        st_send[h] = tn(k_ref[:, c], v_ref[:, c]).astype(BF16)
    for i, r in enumerate(near):
        send(KS, i, st_send.at[r], sb.at[p], p, dev_p(r))
    local(KS, st_send.at[p], sb.at[p], p)

    s_id = lax.broadcasted_iota(jnp.int32, (N, N), 0)
    t_id = lax.broadcasted_iota(jnp.int32, (N, N), 1)
    place = jnp.bitwise_xor(s_id, t_id)
    level = jnp.zeros((N, N), jnp.int32)
    for bit in range(7):
        level = level + (place >= 2**bit).astype(jnp.int32)
    lev_ref[...] = jnp.where(s_id <= t_id, level, -1)

    def own_head(h, _):
        c = pl.ds(pl.multiple_of(h * N, N), N)
        q = q_ref[:, c]
        k = k_ref[:, c]
        v = v_ref[:, c]
        g = g_ref[:, c]
        rows = hg[h, 0:8]
        lev = lev_ref[...]
        w = jnp.zeros((N, N), F32)
        for l in range(8):
            w = jnp.where(lev == l, rows[l : l + 1, :], w)
        wg = (w * nt(v, g)).astype(BF16)
        ws = (w * nt(k, q)).astype(BF16)
        kloc[:, c] = nn(wg, q)
        vloc[:, c] = nn(ws, g)
        qloc[:, c] = tn(wg, k)
        return 0

    lax.fori_loop(0, 4, own_head, 0)

    for i, r in enumerate([p] + near):
        arrived(KQ, qb.at[r], r)
        arrived(KG, gb.at[r], r)
        arrived(KT, gtb.at[r], r)
        qt = qb[r].T.astype(F32)
        rows = gtb[r]
        scaled = jnp.concatenate([(qt * rows[l : l + 1, :]).astype(BF16) for l in range(3, 9)], axis=0)
        part = nn(scaled, gb[r])
        if i == 0:
            lacc[...] = part
        elif i < 7:
            lacc[...] += part
        else:
            lbuf[1:7] = (lacc[...] + part).astype(BF16).reshape(6, N, N)
    kept = {}
    for l in range(8, 2, -1):
        kept[l] = []
        @pl.when(flag[l] == 1)
        def _():
            for i, r in enumerate(far):
                send(KL + l - 3, i, lbuf.at[l - 2, rows16(r), :], urecv.at[a, l - 2], a, dev_a(r), kept[l])
            local(KL + l - 3, lbuf.at[l - 2, rows16(a), :], urecv.at[a, l - 2], a)

    states = []
    for r in range(8):
        arrived(KS, sb.at[r], r)
        states.append(sb[r].astype(F32))
    pair = [states[2 * j] + states[2 * j + 1] for j in range(4)]
    quad = [pair[0] + pair[1], pair[2] + pair[3]]
    lbuf[0] = (quad[0] + quad[1]).astype(BF16)
    for i, r in enumerate(far):
        send(KU, i, lbuf.at[0, rows16(r), :], urecv.at[a, 0], a, dev_a(r))
    local(KU, lbuf.at[0, rows16(a), :], urecv.at[a, 0], a)

    lax.fori_loop(4, HEADS, own_head, 0)

    lows = {}
    for l in range(3, 6):
        for r in range(8):
            if r >> (l - 3) & 1:
                arrived(KL + l - 3, urecv.at[r, l - 2], r)
                lows[l, r] = urecv[r, l - 2].astype(F32)
    for l in range(6, 9):
        @pl.when(flag[l] == 1)
        def _():
            total = zero
            for r in range(8):
                arrived(KL + l - 3, urecv.at[r, l - 2], r)
                total = total + urecv[r, l - 2].astype(F32)
            bsend[l - 5] = total
    down = []
    for r in range(8):
        down.append([])
        @pl.when(r < y)
        def _():
            high = jnp.where(y // 4 != r // 4, 3, jnp.where(y // 2 != r // 2, 2, 1))
            send(KB, r, bsend.at[high], brecv.at[y], y, dev_y(r), down[r])
    l4 = {3: lows[4, 2] + lows[4, 3], 7: lows[4, 6] + lows[4, 7]}
    l5 = (lows[5, 4] + lows[5, 5]) + (lows[5, 6] + lows[5, 7])
    dmid = []
    for r in range(8):
        acc = zero
        if not r & 1:
            acc = acc + lows[3, r + 1]
        if not r & 2:
            acc = acc + l4[r | 3]
        if not r & 4:
            acc = acc + l5
        dmid.append(acc)

    tops = []
    for r in range(8):
        arrived(KU, urecv.at[r, 0], r)
        tops.append(urecv[r, 0].astype(F32))
    tpair = [tops[2 * j] + tops[2 * j + 1] for j in range(4)]
    tquad = [tpair[0] + tpair[1], tpair[2] + tpair[3]]
    bsend[0] = tquad[0] + tquad[1]
    up = []
    for r in range(8):
        up.append([])
        @pl.when(r > y)
        def _():
            send(KB, r, bsend.at[0], brecv.at[y], y, dev_y(r), up[r])
    for r in range(8):
        if r & 1:
            vsend[r, 0] = tops[r - 1].astype(BF16)
        if r & 2:
            vsend[r, 1] = tpair[(r >> 1) ^ 1].astype(BF16)
        if r & 4:
            vsend[r, 2] = tquad[0].astype(BF16)
    side = {}
    for i, r in enumerate(far):
        for l in range(3):
            side[i, l] = []
            @pl.when(r // 2**l % 2 == 1)
            def _():
                send(KV + l, i, vsend.at[r, l], rbuf.at[l, rows16(a), :], a, dev_a(r), side[i, l])
    for l in range(3):
        @pl.when(flag[3 + l] == 1)
        def _():
            local(KV + l, vsend.at[a, l], rbuf.at[l, rows16(a), :], a)

    low = {}
    for r in range(1, 8):
        qt = qb[r].T.astype(F32)
        rows = gtb[r]
        for l in range(3):
            if r >> l & 1:
                part = nn((qt * rows[l : l + 1, :]).astype(BF16), gb[r])
                key = (l, r >> l)
                low[key] = low[key] + part if key in low else part
    for b in range(8):
        acc = jnp.zeros((N, N), F32)
        for l in range(3):
            if not b >> l & 1:
                acc = acc + low[(l, (b >> l) ^ 1)]
        dacc[b] = acc
    pair = [sb[2 * j].astype(F32) + sb[2 * j + 1].astype(F32) for j in range(4)]
    for b in range(8):
        acc = jnp.zeros((N, N), F32)
        rows = gtb[b]
        for l in range(3):
            if b >> l & 1:
                other = (b >> l) ^ 1
                if l == 0:
                    left = sb[other]
                elif l == 1:
                    left = pair[other].astype(BF16)
                else:
                    left = (pair[0] + pair[1]).astype(BF16)
                acc = acc + rows[l : l + 1, :] * nt(left, gb[b])
        ctr[b] = acc

    ysum[...] = jnp.zeros((4, 16, N), F32)
    for r in range(1, 8):
        @pl.when(r > y)
        def _():
            arrived(KB, brecv.at[r], r)
            ysum[3] += brecv[r]
    dtop = ysum[3]
    for r in range(8):
        wsend[r] = (dmid[r] + dtop).astype(BF16)
    for i, r in enumerate(far):
        send(KW, i, wsend.at[r], rbuf.at[6, rows16(a), :], a, dev_a(r))
    local(KW, wsend.at[a], rbuf.at[6, rows16(a), :], a)

    for r in range(7):
        @pl.when(r < y)
        def _():
            arrived(KB, brecv.at[r], r)
            high = jnp.where(y // 4 != r // 4, 2, jnp.where(y // 2 != r // 2, 1, 0))
            ysum[high] += brecv[r]
    for l in range(3):
        xsend[l] = ysum[l].astype(BF16)
    for l in range(3):
        kept[9 + l] = []
        @pl.when(flag[6 + l] == 1)
        def _():
            for i, r in enumerate(far):
                send(KX + l, i, xsend.at[l], rbuf.at[3 + l, rows16(a), :], a, dev_a(r), kept[9 + l])
            local(KX + l, xsend.at[l], rbuf.at[3 + l, rows16(a), :], a)

    for l in range(3):
        @pl.when(flag[3 + l] == 1)
        def _():
            for r in range(8):
                arrived(KV + l, rbuf.at[l, pl.ds(16 * r, 16), :], r)

    def middle(b, _):
        rows = gtb[b]
        prod = nt(rbuf[0:3].reshape(3 * N, N), gb[b])
        acc = ctr[b]
        for l in range(3):
            acc = acc + rows[3 + l : 4 + l, :] * prod[l * N : (l + 1) * N]
        ctr[b] = acc
        return 0

    lax.fori_loop(0, 8, middle, 0, unroll=2)

    for r in range(8):
        arrived(KW, rbuf.at[6, pl.ds(16 * r, 16), :], r)
    for b in range(8):
        dsend[b] = (dacc[b] + rbuf[6].astype(F32)).astype(BF16)
    for i, r in enumerate(near):
        send(KD, i, dsend.at[r], drecv.at[p], p, dev_p(r))
    local(KD, dsend.at[p], drecv.at[p], p)

    for l in range(3):
        @pl.when(flag[6 + l] == 1)
        def _():
            for r in range(8):
                arrived(KX + l, rbuf.at[3 + l, pl.ds(16 * r, 16), :], r)

    for i, b in enumerate(near + [p]):
        rows = gtb[b]
        prod = nt(rbuf[3:6].reshape(3 * N, N), gb[b])
        acc = ctr[b]
        for l in range(3):
            acc = acc + rows[6 + l : 7 + l, :] * prod[l * N : (l + 1) * N]
        csend[b] = acc.T.astype(BF16)
        if i < 7:
            send(KC, i, csend.at[b], crecv.at[p], p, dev_p(b))
    local(KC, csend.at[p], crecv.at[p], p)

    for h in range(HEADS):
        c = slice(h * N, h * N + N)
        arrived(KD, drecv.at[h], h)
        d = drecv[h]
        ko_ref[:, c] = (kloc[:, c] + nt(v_ref[:, c], d)).astype(BF16)
        vo_ref[:, c] = (vloc[:, c] + nn(k_ref[:, c], d)).astype(BF16)
    for h in range(HEADS):
        c = slice(h * N, h * N + N)
        arrived(KC, crecv.at[h], h)
        qo_ref[:, c] = (qloc[:, c] + crecv[h].astype(F32)).astype(BF16)

    sent(sends)
    for l in range(3, 12):
        @pl.when(flag[l if l < 9 else l - 3] == 1)
        def _():
            sent(kept[l])
    for r in range(8):
        @pl.when(r < y)
        def _():
            sent(down[r])
        @pl.when(r > y)
        def _():
            sent(up[r])
    for i, r in enumerate(far):
        for l in range(3):
            @pl.when(r // 2**l % 2 == 1)
            def _():
                sent(side[i, l])


def write_out(qi, ki, vi, qo, ko, vo, sem):
    copies = [pltpu.make_async_copy(s, d, sem.at[i]) for i, (s, d) in enumerate(((qi, qo), (ki, ko), (vi, vo)))]
    for copy in copies:
        copy.start()
    for copy in copies:
        copy.wait()


def per_device(query_rows, key_rows, value_rows, out_grad, gate_class, gate_table):
    table = gate_table.transpose(1, 2, 0)
    out = jax.ShapeDtypeStruct((N, HEADS * N), BF16)
    vmem = pl.BlockSpec(memory_space=pltpu.VMEM)
    hbm = pl.BlockSpec(memory_space=pltpu.HBM)
    cube = lambda n, dtype: pltpu.VMEM((n, N, N), dtype)
    wide = pltpu.VMEM((N, HEADS * N), F32)
    flat = pltpu.VMEM((N, HEADS * N), BF16)
    outs = pl.pallas_call(
        kernel,
        out_shape=(out, out, out),
        in_specs=[hbm] * 6,
        out_specs=(vmem, vmem, vmem),
        scratch_shapes=[
            flat, flat, flat, flat,
            pltpu.VMEM((1, N), jnp.int32),
            pltpu.VMEM((20, HEADS, 32), F32),
            pltpu.VMEM((20 * HEADS, N), F32),
            pltpu.VMEM((HEADS, 24, N), F32),
            pltpu.VMEM((N, N), jnp.int32),
            cube(8, BF16), cube(8, BF16), cube(8, BF16), cube(8, BF16),
            pltpu.VMEM((8, 16, N), F32),
            pltpu.VMEM((6 * N, N), F32),
            wide, wide, wide,
            cube(7, BF16),
            pltpu.VMEM((8, 7, 16, N), BF16),
            pltpu.VMEM((4, 16, N), F32),
            pltpu.VMEM((8, 16, N), F32),
            pltpu.VMEM((4, 16, N), F32),
            pltpu.VMEM((8, 3, 16, N), BF16),
            pltpu.VMEM((8, 16, N), BF16),
            pltpu.VMEM((3, 16, N), BF16),
            cube(7, BF16),
            cube(8, F32), cube(8, F32),
            cube(8, BF16), cube(8, BF16), cube(8, BF16), cube(8, BF16),
            pltpu.SemaphoreType.DMA((6,)),
            pltpu.SemaphoreType.DMA((KINDS, 8)),
            pltpu.SemaphoreType.DMA((KINDS, 8)),
        ],
        compiler_params=pltpu.CompilerParams(
            collective_id=0, has_side_effects=True, vmem_limit_bytes=40 * 1024 * 1024
        ),
    )(*[pltpu.with_memory_space_constraint(one, pltpu.HBM) for one in (query_rows, key_rows, value_rows, out_grad, gate_class.reshape(1, N), table)])
    return pl.pallas_call(
        write_out,
        out_shape=(out, out, out),
        in_specs=[vmem] * 3,
        out_specs=(hbm, hbm, hbm),
        compiler_params=pltpu.CompilerParams(vmem_limit_bytes=16 * 1024 * 1024),
        scratch_shapes=[pltpu.SemaphoreType.DMA((3,))],
    )(*outs)


def solution(mesh):
    rows = P(("gx", "gy"), None)
    return jax.shard_map(
        per_device,
        mesh=mesh,
        in_specs=(rows, rows, rows, rows, P(("gx", "gy")), P()),
        out_specs=(rows, rows, rows),
        check_vma=False,
    )
```

```python
import jax
import jax.numpy as jnp
from jax import lax
from jax.experimental import pallas as pl
from jax.experimental.pallas import tpu as pltpu
from jax.sharding import PartitionSpec as P

MESH = pl.DeviceIdType.MESH
F32 = jnp.float32
BF16 = jnp.bfloat16
N = 128
HEADS = 8
KQ, KG, KT, KS, KL, KU, KB, KV, KW, KX, KC, KD = 0, 1, 2, 3, 4, 10, 11, 12, 15, 16, 19, 20
KINDS = 21
NEAR = ((0, 1), (0, 3), (1, 0), (1, 1), (1, 3), (0, 2), (1, 2))
FAR = ((0, 2), (1, 2), (0, 1), (0, 3), (1, 1), (1, 3), (1, 0))


def mm(a, b, ca, cb):
    return lax.dot_general(a, b, (((ca,), (cb,)), ((), ())), preferred_element_type=F32)


def nn(a, b):
    return mm(a, b, 1, 0)


def nt(a, b):
    return mm(a, b, 1, 1)


def tn(a, b):
    return mm(a, b, 0, 0)


def exchange(
    q_hbm, k_hbm, v_hbm, g_hbm, cls_hbm, tab_hbm,
    qb, gb, sb, gtb, lbuf, k_ref, v_ref, qloc, kloc, vloc,
    q_ref, g_ref, cls_ref, tab_ref, gates, hg, lev_ref, st_send, lacc,
    lsem, ssem, rsem,
):
    gx = lax.axis_index("gx")
    gy = lax.axis_index("gy")
    y = gx // 2
    core = gx % 2
    zz = gy // 8
    p = gy % 8
    z0 = p // 4
    x = p % 4
    a = core * 4 + zz
    flag = {3: zz % 2, 4: zz // 2, 5: core, 6: y % 2, 7: y // 2 % 2, 8: y // 4}
    near = [(z0 + dz) % 2 * 4 + (x + dx) % 4 for dz, dx in NEAR]
    far = [(core + dc) % 2 * 4 + (zz + dz) % 4 for dc, dz in FAR]

    def dev_p(r):
        return (gx, zz * 8 + r)

    def dev_a(r):
        return (y * 2 + r // 4, (r % 4) * 8 + p)

    def dev_y(r):
        return (r * 2 + core, gy)

    barrier = pltpu.get_barrier_semaphore()
    for r in near:
        pl.semaphore_signal(barrier, inc=1, device_id=dev_p(r), device_id_type=MESH)

    loads = []
    for i, (src, dst) in enumerate((
        (cls_hbm, cls_ref), (tab_hbm, tab_ref), (q_hbm, q_ref), (g_hbm, g_ref), (k_hbm, k_ref), (v_hbm, v_ref),
    )):
        loads.append(pltpu.make_async_copy(src, dst, lsem.at[i]))
        loads[-1].start()

    sends = []

    def send(kind, i, src, dst, slot, dev, keep=sends):
        pltpu.make_async_remote_copy(
            src_ref=src, dst_ref=dst, send_sem=ssem.at[kind, i], recv_sem=rsem.at[kind, slot],
            device_id=dev, device_id_type=MESH,
        ).start()
        keep.append((kind, i))

    def sent(done):
        for kind, i in done:
            if kind < KL and kind != KT or kind >= KC:
                like = qb.at[0]
            elif kind == KT:
                like = gtb.at[0]
            pltpu.make_async_copy(like, like, ssem.at[kind, i]).wait()

    def local(kind, src, dst, slot):
        pltpu.make_async_copy(src, dst, rsem.at[kind, slot]).start()

    def arrived(kind, dst, slot):
        pltpu.make_async_copy(dst, dst, rsem.at[kind, slot]).wait()

    def cols(ref, r):
        return ref.at[:, pl.ds(pl.multiple_of(r * N, N), N)]

    def rows16(r):
        return pl.ds(pl.multiple_of(r * 16, 16), 16)

    loads[0].wait()
    loads[1].wait()
    classes = lax.broadcasted_iota(jnp.int32, (32, N), 0)
    onehot = (classes == cls_ref[...]).astype(F32)
    gates[...] = lax.dot_general(
        tab_ref[...].reshape(20 * HEADS, 32), onehot, (((1,), (0,)), ((), ())),
        precision=lax.Precision.HIGHEST, preferred_element_type=F32,
    )
    for h in range(HEADS):
        hg[h, 0:20] = gates[pl.ds(h, 20, stride=HEADS), :]
        hg[h, 20:24] = jnp.zeros((4, N), F32)
    loads[2].wait()
    loads[3].wait()

    pl.semaphore_wait(barrier, 7)

    for i, r in enumerate(near):
        send(KQ, i, cols(q_ref, r), qb.at[p], p, dev_p(r))
        send(KG, i, cols(g_ref, r), gb.at[p], p, dev_p(r))
        send(KT, i, hg.at[r, pl.ds(8, 16)], gtb.at[p], p, dev_p(r))
    local(KQ, cols(q_ref, p), qb.at[p], p)
    local(KG, cols(g_ref, p), gb.at[p], p)
    local(KT, hg.at[p, pl.ds(8, 16)], gtb.at[p], p)

    loads[4].wait()
    loads[5].wait()
    for h in range(HEADS):
        c = slice(h * N, h * N + N)
        st_send[h] = tn(k_ref[:, c], v_ref[:, c]).astype(BF16)
    for i, r in enumerate(near):
        send(KS, i, st_send.at[r], sb.at[p], p, dev_p(r))
    local(KS, st_send.at[p], sb.at[p], p)

    s_id = lax.broadcasted_iota(jnp.int32, (N, N), 0)
    t_id = lax.broadcasted_iota(jnp.int32, (N, N), 1)
    place = jnp.bitwise_xor(s_id, t_id)
    level = jnp.zeros((N, N), jnp.int32)
    for bit in range(7):
        level = level + (place >= 2**bit).astype(jnp.int32)
    lev_ref[...] = jnp.where(s_id <= t_id, level, -1)

    def own_head(h, _):
        c = pl.ds(pl.multiple_of(h * N, N), N)
        q = q_ref[:, c]
        k = k_ref[:, c]
        v = v_ref[:, c]
        g = g_ref[:, c]
        rows = hg[h, 0:8]
        lev = lev_ref[...]
        w = jnp.zeros((N, N), F32)
        for l in range(8):
            w = jnp.where(lev == l, rows[l : l + 1, :], w)
        wg = (w * nt(v, g)).astype(BF16)
        ws = (w * nt(k, q)).astype(BF16)
        kloc[:, c] = nn(wg, q)
        vloc[:, c] = nn(ws, g)
        qloc[:, c] = tn(wg, k)
        return 0

    lax.fori_loop(0, HEADS, own_head, 0)

    for i, r in enumerate([p] + near):
        arrived(KQ, qb.at[r], r)
        arrived(KG, gb.at[r], r)
        arrived(KT, gtb.at[r], r)
        qt = qb[r].T.astype(F32)
        rows = gtb[r]
        scaled = jnp.concatenate([(qt * rows[l : l + 1, :]).astype(BF16) for l in range(3, 9)], axis=0)
        part = nn(scaled, gb[r])
        if i == 0:
            lacc[...] = part
        elif i < 7:
            lacc[...] += part
        else:
            lbuf[...] = (lacc[...] + part).astype(BF16).reshape(6, N, N)
    for r in range(8):
        arrived(KS, sb.at[r], r)
    sent(sends)


def combine(
    qb, gb, sb, gtb, lbuf, k_ref, v_ref, qloc, kloc, vloc,
    qo_ref, ko_ref, vo_ref,
    tsend, urecv, bsend, brecv, ysum, vsend, wsend, xsend, rbuf, ctr, dacc, csend, dsend, crecv, drecv,
    ssem, rsem,
):
    gx = lax.axis_index("gx")
    gy = lax.axis_index("gy")
    y = gx // 2
    core = gx % 2
    zz = gy // 8
    p = gy % 8
    z0 = p // 4
    x = p % 4
    a = core * 4 + zz
    flag = {3: zz % 2, 4: zz // 2, 5: core, 6: y % 2, 7: y // 2 % 2, 8: y // 4}
    near = [(z0 + dz) % 2 * 4 + (x + dx) % 4 for dz, dx in NEAR]
    far = [(core + dc) % 2 * 4 + (zz + dz) % 4 for dc, dz in FAR]

    def dev_p(r):
        return (gx, zz * 8 + r)

    def dev_a(r):
        return (y * 2 + r // 4, (r % 4) * 8 + p)

    def dev_y(r):
        return (r * 2 + core, gy)

    barrier = pltpu.get_barrier_semaphore()
    for i in range(7):
        for dev in (dev_a(far[i]), dev_y((y + i + 1) % 8), dev_p(near[i])):
            pl.semaphore_signal(barrier, inc=1, device_id=dev, device_id_type=MESH)

    sends = []

    def send(kind, i, src, dst, slot, dev, keep=sends):
        pltpu.make_async_remote_copy(
            src_ref=src, dst_ref=dst, send_sem=ssem.at[kind, i], recv_sem=rsem.at[kind, slot],
            device_id=dev, device_id_type=MESH,
        ).start()
        keep.append((kind, i))

    def sent(done):
        for kind, i in done:
            if kind >= KC:
                like = csend.at[0]
            elif kind == KB:
                like = brecv.at[0]
            else:
                like = urecv.at[0, 0]
            pltpu.make_async_copy(like, like, ssem.at[kind, i]).wait()

    def local(kind, src, dst, slot):
        pltpu.make_async_copy(src, dst, rsem.at[kind, slot]).start()

    def arrived(kind, dst, slot):
        pltpu.make_async_copy(dst, dst, rsem.at[kind, slot]).wait()

    def cols(ref, r):
        return ref.at[:, pl.ds(pl.multiple_of(r * N, N), N)]

    def rows16(r):
        return pl.ds(pl.multiple_of(r * 16, 16), 16)

    zero = jnp.zeros((16, N), F32)
    for l in range(3, 9):
        @pl.when(flag[l] == 0)
        def _():
            rbuf[l - 3] = jnp.zeros((N, N), BF16)
    states = []
    for r in range(8):
        states.append(sb[r].astype(F32))
    pair = [states[2 * j] + states[2 * j + 1] for j in range(4)]
    quad = [pair[0] + pair[1], pair[2] + pair[3]]
    tsend[...] = (quad[0] + quad[1]).astype(BF16)
    pl.semaphore_wait(barrier, 21)

    kept = {}
    for l in range(8, 2, -1):
        kept[l] = []
        @pl.when(flag[l] == 1)
        def _():
            for i, r in enumerate(far):
                send(KL + l - 3, i, lbuf.at[l - 3, rows16(r), :], urecv.at[a, l - 2], a, dev_a(r), kept[l])
            local(KL + l - 3, lbuf.at[l - 3, rows16(a), :], urecv.at[a, l - 2], a)

    for i, r in enumerate(far):
        send(KU, i, tsend.at[rows16(r), :], urecv.at[a, 0], a, dev_a(r))
    local(KU, tsend.at[rows16(a), :], urecv.at[a, 0], a)


    low = {}
    for r in range(1, 8):
        qt = qb[r].T.astype(F32)
        rows = gtb[r]
        for l in range(3):
            if r >> l & 1:
                part = nn((qt * rows[l : l + 1, :]).astype(BF16), gb[r])
                key = (l, r >> l)
                low[key] = low[key] + part if key in low else part
    for b in range(8):
        acc = jnp.zeros((N, N), F32)
        for l in range(3):
            if not b >> l & 1:
                acc = acc + low[(l, (b >> l) ^ 1)]
        dacc[b] = acc
    pair = [sb[2 * j].astype(F32) + sb[2 * j + 1].astype(F32) for j in range(4)]
    for b in range(8):
        acc = jnp.zeros((N, N), F32)
        rows = gtb[b]
        for l in range(3):
            if b >> l & 1:
                other = (b >> l) ^ 1
                if l == 0:
                    left = sb[other]
                elif l == 1:
                    left = pair[other].astype(BF16)
                else:
                    left = (pair[0] + pair[1]).astype(BF16)
                acc = acc + rows[l : l + 1, :] * nt(left, gb[b])
        ctr[b] = acc

    lows = {}
    for l in range(3, 6):
        for r in range(8):
            if r >> (l - 3) & 1:
                arrived(KL + l - 3, urecv.at[r, l - 2], r)
                lows[l, r] = urecv[r, l - 2].astype(F32)
    for l in range(6, 9):
        @pl.when(flag[l] == 1)
        def _():
            total = zero
            for r in range(8):
                arrived(KL + l - 3, urecv.at[r, l - 2], r)
                total = total + urecv[r, l - 2].astype(F32)
            bsend[l - 5] = total
    down = []
    for r in range(8):
        down.append([])
        @pl.when(r < y)
        def _():
            high = jnp.where(y // 4 != r // 4, 3, jnp.where(y // 2 != r // 2, 2, 1))
            send(KB, r, bsend.at[high], brecv.at[y], y, dev_y(r), down[r])
    l4 = {3: lows[4, 2] + lows[4, 3], 7: lows[4, 6] + lows[4, 7]}
    l5 = (lows[5, 4] + lows[5, 5]) + (lows[5, 6] + lows[5, 7])
    dmid = []
    for r in range(8):
        acc = zero
        if not r & 1:
            acc = acc + lows[3, r + 1]
        if not r & 2:
            acc = acc + l4[r | 3]
        if not r & 4:
            acc = acc + l5
        dmid.append(acc)

    tops = []
    for r in range(8):
        arrived(KU, urecv.at[r, 0], r)
        tops.append(urecv[r, 0].astype(F32))
    tpair = [tops[2 * j] + tops[2 * j + 1] for j in range(4)]
    tquad = [tpair[0] + tpair[1], tpair[2] + tpair[3]]
    bsend[0] = tquad[0] + tquad[1]
    up = []
    for r in range(8):
        up.append([])
        @pl.when(r > y)
        def _():
            send(KB, r, bsend.at[0], brecv.at[y], y, dev_y(r), up[r])
    for r in range(8):
        if r & 1:
            vsend[r, 0] = tops[r - 1].astype(BF16)
        if r & 2:
            vsend[r, 1] = tpair[(r >> 1) ^ 1].astype(BF16)
        if r & 4:
            vsend[r, 2] = tquad[0].astype(BF16)
    side = {}
    for i, r in enumerate(far):
        for l in range(3):
            side[i, l] = []
            @pl.when(r // 2**l % 2 == 1)
            def _():
                send(KV + l, i, vsend.at[r, l], rbuf.at[l, rows16(a), :], a, dev_a(r), side[i, l])
    for l in range(3):
        @pl.when(flag[3 + l] == 1)
        def _():
            local(KV + l, vsend.at[a, l], rbuf.at[l, rows16(a), :], a)

    ysum[...] = jnp.zeros((4, 16, N), F32)
    for r in range(1, 8):
        @pl.when(r > y)
        def _():
            arrived(KB, brecv.at[r], r)
            ysum[3] += brecv[r]
    dtop = ysum[3]
    for r in range(8):
        wsend[r] = (dmid[r] + dtop).astype(BF16)
    for i, r in enumerate(far):
        send(KW, i, wsend.at[r], rbuf.at[6, rows16(a), :], a, dev_a(r))
    local(KW, wsend.at[a], rbuf.at[6, rows16(a), :], a)

    for r in range(7):
        @pl.when(r < y)
        def _():
            arrived(KB, brecv.at[r], r)
            high = jnp.where(y // 4 != r // 4, 2, jnp.where(y // 2 != r // 2, 1, 0))
            ysum[high] += brecv[r]
    for l in range(3):
        xsend[l] = ysum[l].astype(BF16)
    for l in range(3):
        kept[9 + l] = []
        @pl.when(flag[6 + l] == 1)
        def _():
            for i, r in enumerate(far):
                send(KX + l, i, xsend.at[l], rbuf.at[3 + l, rows16(a), :], a, dev_a(r), kept[9 + l])
            local(KX + l, xsend.at[l], rbuf.at[3 + l, rows16(a), :], a)

    for l in range(3):
        @pl.when(flag[3 + l] == 1)
        def _():
            for r in range(8):
                arrived(KV + l, rbuf.at[l, pl.ds(16 * r, 16), :], r)

    def middle(b, _):
        rows = gtb[b]
        prod = nt(rbuf[0:3].reshape(3 * N, N), gb[b])
        acc = ctr[b]
        for l in range(3):
            acc = acc + rows[3 + l : 4 + l, :] * prod[l * N : (l + 1) * N]
        ctr[b] = acc
        return 0

    lax.fori_loop(0, 8, middle, 0, unroll=2)

    for r in range(8):
        arrived(KW, rbuf.at[6, pl.ds(16 * r, 16), :], r)
    for b in range(8):
        dsend[b] = (dacc[b] + rbuf[6].astype(F32)).astype(BF16)
    for i, r in enumerate(near):
        send(KD, i, dsend.at[r], drecv.at[p], p, dev_p(r))
    local(KD, dsend.at[p], drecv.at[p], p)

    for l in range(3):
        @pl.when(flag[6 + l] == 1)
        def _():
            for r in range(8):
                arrived(KX + l, rbuf.at[3 + l, pl.ds(16 * r, 16), :], r)

    for i, b in enumerate(near + [p]):
        rows = gtb[b]
        prod = nt(rbuf[3:6].reshape(3 * N, N), gb[b])
        acc = ctr[b]
        for l in range(3):
            acc = acc + rows[6 + l : 7 + l, :] * prod[l * N : (l + 1) * N]
        csend[b] = acc.T.astype(BF16)
        if i < 7:
            send(KC, i, csend.at[b], crecv.at[p], p, dev_p(b))
    local(KC, csend.at[p], crecv.at[p], p)

    for h in range(HEADS):
        c = slice(h * N, h * N + N)
        arrived(KD, drecv.at[h], h)
        d = drecv[h]
        ko_ref[:, c] = (kloc[:, c] + nt(v_ref[:, c], d)).astype(BF16)
        vo_ref[:, c] = (vloc[:, c] + nn(k_ref[:, c], d)).astype(BF16)
    for h in range(HEADS):
        c = slice(h * N, h * N + N)
        arrived(KC, crecv.at[h], h)
        qo_ref[:, c] = (qloc[:, c] + crecv[h].astype(F32)).astype(BF16)

    sent(sends)
    for l in range(3, 12):
        @pl.when(flag[l if l < 9 else l - 3] == 1)
        def _():
            sent(kept[l])
    for r in range(8):
        @pl.when(r < y)
        def _():
            sent(down[r])
        @pl.when(r > y)
        def _():
            sent(up[r])
    for i, r in enumerate(far):
        for l in range(3):
            @pl.when(r // 2**l % 2 == 1)
            def _():
                sent(side[i, l])


def write_out(qi, ki, vi, qo, ko, vo, sem):
    copies = [pltpu.make_async_copy(s, d, sem.at[i]) for i, (s, d) in enumerate(((qi, qo), (ki, ko), (vi, vo)))]
    for copy in copies:
        copy.start()
    for copy in copies:
        copy.wait()


def per_device(query_rows, key_rows, value_rows, out_grad, gate_class, gate_table):
    table = gate_table.transpose(1, 2, 0)
    out = jax.ShapeDtypeStruct((N, HEADS * N), BF16)
    loc = jax.ShapeDtypeStruct((N, HEADS * N), F32)
    eight = jax.ShapeDtypeStruct((8, N, N), BF16)
    vmem = pl.BlockSpec(memory_space=pltpu.VMEM)
    hbm = pl.BlockSpec(memory_space=pltpu.HBM)
    cube = lambda n, dtype: pltpu.VMEM((n, N, N), dtype)
    flat = pltpu.VMEM((N, HEADS * N), BF16)
    args = (query_rows, key_rows, value_rows, out_grad, gate_class.reshape(1, N), table)
    held = pl.pallas_call(
        exchange,
        out_shape=(
            eight, eight, eight, jax.ShapeDtypeStruct((8, 16, N), F32),
            jax.ShapeDtypeStruct((6, N, N), BF16), out, out, loc, loc, loc,
        ),
        in_specs=[hbm] * 6,
        out_specs=(vmem,) * 10,
        scratch_shapes=[
            flat, flat,
            pltpu.VMEM((1, N), jnp.int32),
            pltpu.VMEM((20, HEADS, 32), F32),
            pltpu.VMEM((20 * HEADS, N), F32),
            pltpu.VMEM((HEADS, 24, N), F32),
            pltpu.VMEM((N, N), jnp.int32),
            cube(8, BF16),
            pltpu.VMEM((6 * N, N), F32),
            pltpu.SemaphoreType.DMA((6,)),
            pltpu.SemaphoreType.DMA((4, 8)),
            pltpu.SemaphoreType.DMA((4, 8)),
        ],
        compiler_params=pltpu.CompilerParams(
            collective_id=0, has_side_effects=True, vmem_limit_bytes=24 * 1024 * 1024
        ),
    )(*[pltpu.with_memory_space_constraint(one, pltpu.HBM) for one in args])
    outs = pl.pallas_call(
        combine,
        out_shape=(out, out, out),
        in_specs=[vmem] * 10,
        out_specs=(vmem, vmem, vmem),
        scratch_shapes=[
            pltpu.VMEM((N, N), BF16),
            pltpu.VMEM((8, 7, 16, N), BF16),
            pltpu.VMEM((4, 16, N), F32),
            pltpu.VMEM((8, 16, N), F32),
            pltpu.VMEM((4, 16, N), F32),
            pltpu.VMEM((8, 3, 16, N), BF16),
            pltpu.VMEM((8, 16, N), BF16),
            pltpu.VMEM((3, 16, N), BF16),
            cube(7, BF16),
            cube(8, F32), cube(8, F32),
            cube(8, BF16), cube(8, BF16), cube(8, BF16), cube(8, BF16),
            pltpu.SemaphoreType.DMA((KINDS, 8)),
            pltpu.SemaphoreType.DMA((KINDS, 8)),
        ],
        compiler_params=pltpu.CompilerParams(
            collective_id=1, has_side_effects=True, vmem_limit_bytes=24 * 1024 * 1024
        ),
    )(*held)
    return pl.pallas_call(
        write_out,
        out_shape=(out, out, out),
        in_specs=[vmem] * 3,
        out_specs=(hbm, hbm, hbm),
        compiler_params=pltpu.CompilerParams(vmem_limit_bytes=16 * 1024 * 1024),
        scratch_shapes=[pltpu.SemaphoreType.DMA((3,))],
    )(*outs)


def solution(mesh):
    rows = P(("gx", "gy"), None)
    return jax.shard_map(
        per_device,
        mesh=mesh,
        in_specs=(rows, rows, rows, rows, P(("gx", "gy")), P()),
        out_specs=(rows, rows, rows),
        check_vma=False,
    )
```

```python
import jax
import jax.numpy as jnp
from jax import lax
from jax.experimental import pallas as pl
from jax.experimental.pallas import tpu as pltpu
from jax.sharding import PartitionSpec as P

MESH = pl.DeviceIdType.MESH
F32 = jnp.float32
BF16 = jnp.bfloat16
N = 128
HEADS = 8
KQ, KG, KT, KS, KL, KU, KB, KV, KW, KX, KC, KD = 0, 1, 2, 3, 4, 10, 11, 12, 15, 16, 19, 20
KH = 21
KINDS = 22
NEAR = ((0, 1), (0, 3), (1, 0), (1, 1), (1, 3), (0, 2), (1, 2))
FAR = ((0, 2), (1, 2), (0, 1), (0, 3), (1, 1), (1, 3), (1, 0))


def mm(a, b, ca, cb):
    return lax.dot_general(a, b, (((ca,), (cb,)), ((), ())), preferred_element_type=F32)


def nn(a, b):
    return mm(a, b, 1, 0)


def nt(a, b):
    return mm(a, b, 1, 1)


def tn(a, b):
    return mm(a, b, 0, 0)


def kernel(
    q_hbm, k_hbm, v_hbm, g_hbm, cls_hbm, tab_hbm,
    qo_ref, ko_ref, vo_ref,
    q_ref, k_ref, v_ref, g_ref, cls_ref, tab_ref,
    gates, hg, lev_ref, st_send, qt_send, qb, gb, sb, gtb, lacc, qloc, kloc, vloc,
    tsend, lbuf, urecv, bsend, brecv, ysum, vsend, wsend, xsend, rbuf, ctr, dacc, csend, dsend, crecv, drecv,
    lsem, ssem, rsem,
):
    gx = lax.axis_index("gx")
    gy = lax.axis_index("gy")
    y = gx // 2
    core = gx % 2
    zz = gy // 8
    p = gy % 8
    z0 = p // 4
    x = p % 4
    a = core * 4 + zz
    flag = {3: zz % 2, 4: zz // 2, 5: core, 6: y % 2, 7: y // 2 % 2, 8: y // 4}
    near = [(z0 + dz) % 2 * 4 + (x + dx) % 4 for dz, dx in NEAR]
    far = [(core + dc) % 2 * 4 + (zz + dz) % 4 for dc, dz in FAR]

    def dev_p(r):
        return (gx, zz * 8 + r)

    def dev_a(r):
        return (y * 2 + r // 4, (r % 4) * 8 + p)

    def dev_y(r):
        return (r * 2 + core, gy)

    barrier = pltpu.get_barrier_semaphore()
    for i in range(7):
        for dev in (dev_p(near[i]), dev_a(far[i]), dev_y((y + i + 1) % 8)):
            pl.semaphore_signal(barrier, inc=1, device_id=dev, device_id_type=MESH)

    loads = []
    for i, (src, dst) in enumerate((
        (cls_hbm, cls_ref), (tab_hbm, tab_ref), (q_hbm, q_ref), (g_hbm, g_ref), (k_hbm, k_ref), (v_hbm, v_ref),
    )):
        loads.append(pltpu.make_async_copy(src, dst, lsem.at[i]))
        loads[-1].start()

    sends = []

    def send(kind, i, src, dst, slot, dev, keep=sends):
        pltpu.make_async_remote_copy(
            src_ref=src, dst_ref=dst, send_sem=ssem.at[kind, i], recv_sem=rsem.at[kind, slot],
            device_id=dev, device_id_type=MESH,
        ).start()
        keep.append((kind, i))

    def sent(done):
        for kind, i in done:
            if kind in (KQ, KH):
                like = qb.at[0, pl.ds(0, 64)]
            elif kind in (KG, KS, KC, KD):
                like = qb.at[0]
            elif kind == KT:
                like = gtb.at[0]
            elif kind == KB:
                like = brecv.at[0]
            else:
                like = urecv.at[0, 0]
            pltpu.make_async_copy(like, like, ssem.at[kind, i]).wait()

    def local(kind, src, dst, slot):
        pltpu.make_async_copy(src, dst, rsem.at[kind, slot]).start()

    def arrived(kind, dst, slot):
        pltpu.make_async_copy(dst, dst, rsem.at[kind, slot]).wait()

    def cols(ref, r):
        return ref.at[:, pl.ds(pl.multiple_of(r * N, N), N)]

    def rows16(r):
        return pl.ds(pl.multiple_of(r * 16, 16), 16)

    zero = jnp.zeros((16, N), F32)
    for l in range(3, 9):
        @pl.when(flag[l] == 0)
        def _():
            rbuf[l - 3] = jnp.zeros((N, N), BF16)
    loads[0].wait()
    loads[1].wait()
    classes = lax.broadcasted_iota(jnp.int32, (32, N), 0)
    onehot = (classes == cls_ref[...]).astype(F32)
    gates[...] = lax.dot_general(
        tab_ref[...].reshape(20 * HEADS, 32), onehot, (((1,), (0,)), ((), ())),
        precision=lax.Precision.HIGHEST, preferred_element_type=F32,
    )
    for h in range(HEADS):
        hg[h, 0:20] = gates[pl.ds(h, 20, stride=HEADS), :]
        hg[h, 20:24] = jnp.zeros((4, N), F32)
    loads[2].wait()
    loads[4].wait()
    loads[5].wait()
    for h in range(HEADS):
        c = slice(h * N, h * N + N)
        st_send[h] = tn(k_ref[:, c], v_ref[:, c]).astype(BF16)
        qt_send[h] = q_ref[:, c].T
    loads[3].wait()

    pl.semaphore_wait(barrier, 21)

    half = (pl.ds(0, 64), pl.ds(64, 64))
    for i, r in enumerate(near):
        send(KS, i, st_send.at[r], sb.at[p], p, dev_p(r))
    for i, r in enumerate(near):
        send(KG, i, cols(g_ref, r), gb.at[p], p, dev_p(r))
        send(KT, i, hg.at[r, pl.ds(8, 16)], gtb.at[p], p, dev_p(r))
    for kind, part in ((KQ, half[0]), (KH, half[1])):
        for i, r in enumerate(near):
            send(kind, i, qt_send.at[r, part], qb.at[p, part], p, dev_p(r))
        local(kind, qt_send.at[p, part], qb.at[p, part], p)
    local(KS, st_send.at[p], sb.at[p], p)
    local(KG, cols(g_ref, p), gb.at[p], p)
    local(KT, hg.at[p, pl.ds(8, 16)], gtb.at[p], p)

    s_id = lax.broadcasted_iota(jnp.int32, (N, N), 0)
    t_id = lax.broadcasted_iota(jnp.int32, (N, N), 1)
    place = jnp.bitwise_xor(s_id, t_id)
    level = jnp.zeros((N, N), jnp.int32)
    for bit in range(7):
        level = level + (place >= 2**bit).astype(jnp.int32)
    lev_ref[...] = jnp.where(s_id <= t_id, level, -1)

    def own_head(h, _):
        c = pl.ds(pl.multiple_of(h * N, N), N)
        q = q_ref[:, c]
        k = k_ref[:, c]
        v = v_ref[:, c]
        g = g_ref[:, c]
        rows = hg[h, 0:8]
        lev = lev_ref[...]
        w = jnp.zeros((N, N), F32)
        for l in range(8):
            w = jnp.where(lev == l, rows[l : l + 1, :], w)
        wg = (w * nt(v, g)).astype(BF16)
        ws = (w * nt(k, q)).astype(BF16)
        kloc[:, c] = nn(wg, q)
        vloc[:, c] = nn(ws, g)
        qloc[:, c] = tn(wg, k)
        return 0

    lax.fori_loop(0, HEADS, own_head, 0)

    states = []
    for r in range(8):
        arrived(KS, sb.at[r], r)
        states.append(sb[r].astype(F32))
    pair = [states[2 * j] + states[2 * j + 1] for j in range(4)]
    tsend[...] = ((pair[0] + pair[1]) + (pair[2] + pair[3])).astype(BF16)
    for i, r in enumerate(far):
        send(KU, i, tsend.at[rows16(r), :], urecv.at[a, 0], a, dev_a(r))
    local(KU, tsend.at[rows16(a), :], urecv.at[a, 0], a)

    for part in range(2):
        for i, r in enumerate([p] + near):
            if part == 0:
                arrived(KG, gb.at[r], r)
                arrived(KT, gtb.at[r], r)
            arrived((KQ, KH)[part], qb.at[r, half[part]], r)
            qt = qb[r, part * 64 : part * 64 + 64].astype(F32)
            rows = gtb[r]
            scaled = jnp.concatenate([(qt * rows[l : l + 1, :]).astype(BF16) for l in range(3, 9)], axis=0)
            prod = nn(scaled, gb[r])
            if i == 0:
                lacc[...] = prod
            elif i < 7:
                lacc[...] += prod
            else:
                lbuf[:, part * 64 : part * 64 + 64] = (lacc[...] + prod).astype(BF16).reshape(6, 64, N)
        for l in range(8, 2, -1):
            @pl.when(flag[l] == 1)
            def _():
                for dz in (2, 1, 3):
                    r = part * 4 + (zz + dz) % 4
                    send(KL + l - 3, part * 4 + dz, lbuf.at[l - 3, rows16(r), :], urecv.at[a, l - 2], a, dev_a(r), [])
                @pl.when(core == part)
                def _():
                    local(KL + l - 3, lbuf.at[l - 3, rows16(a), :], urecv.at[a, l - 2], a)
                @pl.when(core != part)
                def _():
                    r = part * 4 + zz
                    send(KL + l - 3, part * 4, lbuf.at[l - 3, rows16(r), :], urecv.at[a, l - 2], a, dev_a(r), [])
    kept = {}

    ysum[...] = jnp.zeros((4, 16, N), F32)
    tops = []
    for r in range(8):
        arrived(KU, urecv.at[r, 0], r)
        tops.append(urecv[r, 0].astype(F32))
    tpair = [tops[2 * j] + tops[2 * j + 1] for j in range(4)]
    tquad = [tpair[0] + tpair[1], tpair[2] + tpair[3]]
    bsend[0] = tquad[0] + tquad[1]
    up = []
    for r in range(8):
        up.append([])
        @pl.when(r > y)
        def _():
            send(KB, r, bsend.at[0], brecv.at[y], y, dev_y(r), up[r])
    for r in range(8):
        if r & 1:
            vsend[r, 0] = tops[r - 1].astype(BF16)
        if r & 2:
            vsend[r, 1] = tpair[(r >> 1) ^ 1].astype(BF16)
        if r & 4:
            vsend[r, 2] = tquad[0].astype(BF16)
    side = {}
    for i, r in enumerate(far):
        for l in range(3):
            side[i, l] = []
            @pl.when(r // 2**l % 2 == 1)
            def _():
                send(KV + l, i, vsend.at[r, l], rbuf.at[l, rows16(a), :], a, dev_a(r), side[i, l])
    for l in range(3):
        @pl.when(flag[3 + l] == 1)
        def _():
            local(KV + l, vsend.at[a, l], rbuf.at[l, rows16(a), :], a)

    low = {}
    for r in range(1, 8):
        qt = qb[r].astype(F32)
        rows = gtb[r]
        for l in range(3):
            if r >> l & 1:
                part = nn((qt * rows[l : l + 1, :]).astype(BF16), gb[r])
                key = (l, r >> l)
                low[key] = low[key] + part if key in low else part
    for b in range(8):
        acc = jnp.zeros((N, N), F32)
        for l in range(3):
            if not b >> l & 1:
                acc = acc + low[(l, (b >> l) ^ 1)]
        dacc[b] = acc
    pair = [sb[2 * j].astype(F32) + sb[2 * j + 1].astype(F32) for j in range(4)]
    for b in range(8):
        acc = jnp.zeros((N, N), F32)
        rows = gtb[b]
        for l in range(3):
            if b >> l & 1:
                other = (b >> l) ^ 1
                if l == 0:
                    left = sb[other]
                elif l == 1:
                    left = pair[other].astype(BF16)
                else:
                    left = (pair[0] + pair[1]).astype(BF16)
                acc = acc + rows[l : l + 1, :] * nt(left, gb[b])
        ctr[b] = acc

    for r in range(7):
        @pl.when(r < y)
        def _():
            arrived(KB, brecv.at[r], r)
            high = jnp.where(y // 4 != r // 4, 2, jnp.where(y // 2 != r // 2, 1, 0))
            ysum[high] += brecv[r]
    for l in range(3):
        xsend[l] = ysum[l].astype(BF16)
    for l in range(3):
        kept[9 + l] = []
        @pl.when(flag[6 + l] == 1)
        def _():
            for i, r in enumerate(far):
                send(KX + l, i, xsend.at[l], rbuf.at[3 + l, rows16(a), :], a, dev_a(r), kept[9 + l])
            local(KX + l, xsend.at[l], rbuf.at[3 + l, rows16(a), :], a)

    lows = {}
    for l in range(3, 6):
        for r in range(8):
            if r >> (l - 3) & 1:
                arrived(KL + l - 3, urecv.at[r, l - 2], r)
                lows[l, r] = urecv[r, l - 2].astype(F32)
    for l in range(6, 9):
        @pl.when(flag[l] == 1)
        def _():
            total = zero
            for r in range(8):
                arrived(KL + l - 3, urecv.at[r, l - 2], r)
                total = total + urecv[r, l - 2].astype(F32)
            bsend[l - 5] = total
    down = []
    for r in range(8):
        down.append([])
        @pl.when(r < y)
        def _():
            high = jnp.where(y // 4 != r // 4, 3, jnp.where(y // 2 != r // 2, 2, 1))
            send(KB, r, bsend.at[high], brecv.at[y], y, dev_y(r), down[r])
    l4 = {3: lows[4, 2] + lows[4, 3], 7: lows[4, 6] + lows[4, 7]}
    l5 = (lows[5, 4] + lows[5, 5]) + (lows[5, 6] + lows[5, 7])
    dmid = []
    for r in range(8):
        acc = zero
        if not r & 1:
            acc = acc + lows[3, r + 1]
        if not r & 2:
            acc = acc + l4[r | 3]
        if not r & 4:
            acc = acc + l5
        dmid.append(acc)

    for l in range(3):
        @pl.when(flag[3 + l] == 1)
        def _():
            for r in range(8):
                arrived(KV + l, rbuf.at[l, pl.ds(16 * r, 16), :], r)

    def middle(b, _):
        rows = gtb[b]
        prod = nt(rbuf[0:3].reshape(3 * N, N), gb[b])
        acc = ctr[b]
        for l in range(3):
            acc = acc + rows[3 + l : 4 + l, :] * prod[l * N : (l + 1) * N]
        ctr[b] = acc
        return 0

    lax.fori_loop(0, 8, middle, 0, unroll=2)

    for r in range(1, 8):
        @pl.when(r > y)
        def _():
            arrived(KB, brecv.at[r], r)
            ysum[3] += brecv[r]
    dtop = ysum[3]
    for r in range(8):
        wsend[r] = (dmid[r] + dtop).astype(BF16)
    for i, r in enumerate(far):
        send(KW, i, wsend.at[r], rbuf.at[6, rows16(a), :], a, dev_a(r))
    local(KW, wsend.at[a], rbuf.at[6, rows16(a), :], a)

    for l in range(3):
        @pl.when(flag[6 + l] == 1)
        def _():
            for r in range(8):
                arrived(KX + l, rbuf.at[3 + l, pl.ds(16 * r, 16), :], r)

    for i, b in enumerate(near + [p]):
        rows = gtb[b]
        prod = nt(rbuf[3:6].reshape(3 * N, N), gb[b])
        acc = ctr[b]
        for l in range(3):
            acc = acc + rows[6 + l : 7 + l, :] * prod[l * N : (l + 1) * N]
        csend[b] = acc.T.astype(BF16)
        if i < 7:
            send(KC, i, csend.at[b], crecv.at[p], p, dev_p(b))
    local(KC, csend.at[p], crecv.at[p], p)

    for r in range(8):
        arrived(KW, rbuf.at[6, pl.ds(16 * r, 16), :], r)
    dall = rbuf[6].astype(F32)
    for i, r in enumerate(near):
        dsend[r] = (dacc[r] + dall).astype(BF16)
        send(KD, i, dsend.at[r], drecv.at[p], p, dev_p(r))
    dsend[p] = (dacc[p] + dall).astype(BF16)
    local(KD, dsend.at[p], drecv.at[p], p)

    for r in [p] + near:
        c = pl.ds(pl.multiple_of(r * N, N), N)
        arrived(KC, crecv.at[r], r)
        qo_ref[:, c] = (qloc[:, c] + crecv[r].astype(F32)).astype(BF16)
    for r in [p] + near:
        c = pl.ds(pl.multiple_of(r * N, N), N)
        arrived(KD, drecv.at[r], r)
        d = drecv[r]
        ko_ref[:, c] = (kloc[:, c] + nt(v_ref[:, c], d)).astype(BF16)
        vo_ref[:, c] = (vloc[:, c] + nn(k_ref[:, c], d)).astype(BF16)

    sent(sends)
    for part in range(2):
        for l in range(3, 9):
            @pl.when(flag[l] == 1)
            def _():
                sent([(KL + l - 3, part * 4 + dz) for dz in (1, 2, 3)])
                @pl.when(core != part)
                def _():
                    sent([(KL + l - 3, part * 4)])
    for l in range(9, 12):
        @pl.when(flag[l if l < 9 else l - 3] == 1)
        def _():
            sent(kept[l])
    for r in range(8):
        @pl.when(r < y)
        def _():
            sent(down[r])
        @pl.when(r > y)
        def _():
            sent(up[r])
    for i, r in enumerate(far):
        for l in range(3):
            @pl.when(r // 2**l % 2 == 1)
            def _():
                sent(side[i, l])


def write_out(qi, ki, vi, qo, ko, vo, sem):
    copies = [pltpu.make_async_copy(s, d, sem.at[i]) for i, (s, d) in enumerate(((qi, qo), (ki, ko), (vi, vo)))]
    for copy in copies:
        copy.start()
    for copy in copies:
        copy.wait()


def per_device(query_rows, key_rows, value_rows, out_grad, gate_class, gate_table):
    table = gate_table.transpose(1, 2, 0)
    out = jax.ShapeDtypeStruct((N, HEADS * N), BF16)
    vmem = pl.BlockSpec(memory_space=pltpu.VMEM)
    hbm = pl.BlockSpec(memory_space=pltpu.HBM)
    cube = lambda n, dtype: pltpu.VMEM((n, N, N), dtype)
    wide = pltpu.VMEM((N, HEADS * N), F32)
    flat = pltpu.VMEM((N, HEADS * N), BF16)
    outs = pl.pallas_call(
        kernel,
        out_shape=(out, out, out),
        in_specs=[hbm] * 6,
        out_specs=(vmem, vmem, vmem),
        scratch_shapes=[
            flat, flat, flat, flat,
            pltpu.VMEM((1, N), jnp.int32),
            pltpu.VMEM((20, HEADS, 32), F32),
            pltpu.VMEM((20 * HEADS, N), F32),
            pltpu.VMEM((HEADS, 24, N), F32),
            pltpu.VMEM((N, N), jnp.int32),
            cube(8, BF16), cube(8, BF16), cube(8, BF16), cube(8, BF16), cube(8, BF16),
            pltpu.VMEM((8, 16, N), F32),
            pltpu.VMEM((3 * N, N), F32),
            wide, wide, wide,
            pltpu.VMEM((N, N), BF16),
            cube(6, BF16),
            pltpu.VMEM((8, 7, 16, N), BF16),
            pltpu.VMEM((4, 16, N), F32),
            pltpu.VMEM((8, 16, N), F32),
            pltpu.VMEM((4, 16, N), F32),
            pltpu.VMEM((8, 3, 16, N), BF16),
            pltpu.VMEM((8, 16, N), BF16),
            pltpu.VMEM((3, 16, N), BF16),
            cube(7, BF16),
            cube(8, F32), cube(8, F32),
            cube(8, BF16), cube(8, BF16), cube(8, BF16), cube(8, BF16),
            pltpu.SemaphoreType.DMA((6,)),
            pltpu.SemaphoreType.DMA((KINDS, 8)),
            pltpu.SemaphoreType.DMA((KINDS, 8)),
        ],
        compiler_params=pltpu.CompilerParams(
            collective_id=0, has_side_effects=True, vmem_limit_bytes=40 * 1024 * 1024
        ),
    )(*[pltpu.with_memory_space_constraint(one, pltpu.HBM) for one in (query_rows, key_rows, value_rows, out_grad, gate_class.reshape(1, N), table)])
    return pl.pallas_call(
        write_out,
        out_shape=(out, out, out),
        in_specs=[vmem] * 3,
        out_specs=(hbm, hbm, hbm),
        compiler_params=pltpu.CompilerParams(vmem_limit_bytes=16 * 1024 * 1024),
        scratch_shapes=[pltpu.SemaphoreType.DMA((3,))],
    )(*outs)


def solution(mesh):
    rows = P(("gx", "gy"), None)
    return jax.shard_map(
        per_device,
        mesh=mesh,
        in_specs=(rows, rows, rows, rows, P(("gx", "gy")), P()),
        out_specs=(rows, rows, rows),
        check_vma=False,
    )
```

```python
import jax
import jax.numpy as jnp
from jax import lax
from jax.experimental import pallas as pl
from jax.experimental.pallas import tpu as pltpu
from jax.sharding import PartitionSpec as P

MESH = pl.DeviceIdType.MESH
F32 = jnp.float32
BF16 = jnp.bfloat16
N = 128
HEADS = 8
KS, KG, KT, KQ, KH, KU, KL, KB, KV, KX, KW, KC, KD = range(13)
KINDS = 13
NEAR = ((0, 1), (0, 3), (1, 0), (1, 1), (1, 3), (0, 2), (1, 2))
FAR = ((0, 2), (1, 2), (0, 1), (0, 3), (1, 1), (1, 3), (1, 0))


def mm(a, b, ca, cb):
    return lax.dot_general(a, b, (((ca,), (cb,)), ((), ())), preferred_element_type=F32)


def nn(a, b):
    return mm(a, b, 1, 0)


def nt(a, b):
    return mm(a, b, 1, 1)


def tn(a, b):
    return mm(a, b, 0, 0)


def kernel(
    q_hbm, k_hbm, v_hbm, g_hbm, cls_hbm, tab_hbm,
    qo_ref, ko_ref, vo_ref,
    q_ref, k_ref, v_ref, g_ref, cls_ref, tab_ref,
    gates, hg, lev_ref, st_send, qt_send, qb, gb, sb, gtb, lacc, qloc, kloc, vloc,
    tsend, lbuf, trecv, lrecv, bsend, brecv, ysum, vsend, wsend, xsend, rbuf, ctr, dacc, csend, dsend, crecv, drecv,
    lsem, ssem, rsem,
):
    gx = lax.axis_index("gx")
    gy = lax.axis_index("gy")
    y = gx // 2
    core = gx % 2
    zz = gy // 8
    p = gy % 8
    z0 = p // 4
    x = p % 4
    a = core * 4 + zz
    near = [(z0 + dz) % 2 * 4 + (x + dx) % 4 for dz, dx in NEAR]
    far = [(core + dc) % 2 * 4 + (zz + dz) % 4 for dc, dz in FAR]

    def dev_p(r):
        return (gx, zz * 8 + r)

    def dev_a(r):
        return (y * 2 + r // 4, (r % 4) * 8 + p)

    def dev_y(r):
        return (r * 2 + core, gy)

    barrier = pltpu.get_barrier_semaphore()
    for i in range(7):
        for dev in (dev_p(near[i]), dev_a(far[i]), dev_y((y + i + 1) % 8)):
            pl.semaphore_signal(barrier, inc=1, device_id=dev, device_id_type=MESH)

    loads = []
    for i, (src, dst) in enumerate((
        (cls_hbm, cls_ref), (tab_hbm, tab_ref), (q_hbm, q_ref), (g_hbm, g_ref), (k_hbm, k_ref), (v_hbm, v_ref),
    )):
        loads.append(pltpu.make_async_copy(src, dst, lsem.at[i]))
        loads[-1].start()

    def send(kind, src, dst, slot, dev):
        pltpu.make_async_remote_copy(
            src_ref=src, dst_ref=dst, send_sem=ssem.at[kind], recv_sem=rsem.at[kind, slot],
            device_id=dev, device_id_type=MESH,
        ).start()

    def sent(kind, like):
        pltpu.make_async_copy(like, like, ssem.at[kind]).wait()

    def local(kind, src, dst, slot):
        pltpu.make_async_copy(src, dst, rsem.at[kind, slot]).start()

    def arrived(kind, dst, slot):
        pltpu.make_async_copy(dst, dst, rsem.at[kind, slot]).wait()

    def cols(ref, r):
        return ref.at[:, pl.ds(pl.multiple_of(r * N, N), N)]

    def rows16(r):
        return pl.ds(pl.multiple_of(r * 16, 16), 16)

    zero = jnp.zeros((16, N), F32)
    loads[0].wait()
    loads[1].wait()
    classes = lax.broadcasted_iota(jnp.int32, (32, N), 0)
    onehot = (classes == cls_ref[...]).astype(F32)
    gates[...] = lax.dot_general(
        tab_ref[...].reshape(20 * HEADS, 32), onehot, (((1,), (0,)), ((), ())),
        precision=lax.Precision.HIGHEST, preferred_element_type=F32,
    )
    for h in range(HEADS):
        hg[h, 0:20] = gates[pl.ds(h, 20, stride=HEADS), :]
        hg[h, 20:24] = jnp.zeros((4, N), F32)
    loads[2].wait()
    loads[4].wait()
    loads[5].wait()
    for h in range(HEADS):
        c = slice(h * N, h * N + N)
        st_send[h] = tn(k_ref[:, c], v_ref[:, c]).astype(BF16)
        qt_send[h] = q_ref[:, c].T
    loads[3].wait()

    pl.semaphore_wait(barrier, 21)

    half = (pl.ds(0, 64), pl.ds(64, 64))
    for r in near:
        send(KS, st_send.at[r], sb.at[p], 0, dev_p(r))
    for r in near:
        send(KG, cols(g_ref, r), gb.at[p], p, dev_p(r))
        send(KT, hg.at[r, pl.ds(8, 16)], gtb.at[p], 0, dev_p(r))
    for kind, part in ((KQ, half[0]), (KH, half[1])):
        for r in near:
            send(kind, qt_send.at[r, part], qb.at[p, part], p, dev_p(r))
        local(kind, qt_send.at[p, part], qb.at[p, part], p)
    local(KS, st_send.at[p], sb.at[p], 0)
    local(KG, cols(g_ref, p), gb.at[p], p)
    local(KT, hg.at[p, pl.ds(8, 16)], gtb.at[p], 0)

    s_id = lax.broadcasted_iota(jnp.int32, (N, N), 0)
    t_id = lax.broadcasted_iota(jnp.int32, (N, N), 1)
    place = jnp.bitwise_xor(s_id, t_id)
    level = jnp.zeros((N, N), jnp.int32)
    for bit in range(7):
        level = level + (place >= 2**bit).astype(jnp.int32)
    lev_ref[...] = jnp.where(s_id <= t_id, level, -1)

    def own_head(h, _):
        c = pl.ds(pl.multiple_of(h * N, N), N)
        q = q_ref[:, c]
        k = k_ref[:, c]
        v = v_ref[:, c]
        g = g_ref[:, c]
        rows = hg[h, 0:8]
        lev = lev_ref[...]
        w = jnp.zeros((N, N), F32)
        for l in range(8):
            w = jnp.where(lev == l, rows[l : l + 1, :], w)
        wg = (w * nt(v, g)).astype(BF16)
        ws = (w * nt(k, q)).astype(BF16)
        kloc[:, c] = nn(wg, q)
        vloc[:, c] = nn(ws, g)
        qloc[:, c] = tn(wg, k)
        return 0

    lax.fori_loop(0, HEADS, own_head, 0)

    arrived(KS, sb, 0)
    states = [sb[r].astype(F32) for r in range(8)]
    pair = [states[2 * j] + states[2 * j + 1] for j in range(4)]
    tsend[...] = ((pair[0] + pair[1]) + (pair[2] + pair[3])).astype(BF16)
    for r in far:
        send(KU, tsend.at[rows16(r), :], trecv.at[a], 0, dev_a(r))
    local(KU, tsend.at[rows16(a), :], trecv.at[a], 0)

    arrived(KT, gtb, 0)
    for part in range(2):
        for i, r in enumerate([p] + near):
            if part == 0:
                arrived(KG, gb.at[r], r)
            arrived((KQ, KH)[part], qb.at[r, half[part]], r)
            qt = qb[r, part * 64 : part * 64 + 64].astype(F32)
            rows = gtb[r]
            scaled = jnp.concatenate([(qt * rows[l : l + 1, :]).astype(BF16) for l in range(3, 9)], axis=0)
            prod = nn(scaled, gb[r])
            if i == 0:
                lacc[...] = prod
            elif i < 7:
                lacc[...] += prod
            else:
                lbuf[:, part * 64 : part * 64 + 64] = (lacc[...] + prod).astype(BF16).reshape(6, 64, N)
        for dz in (2, 1, 3):
            r = part * 4 + (zz + dz) % 4
            send(KL, lbuf.at[:, rows16(r), :], lrecv.at[a], 0, dev_a(r))
        @pl.when(core == part)
        def _():
            local(KL, lbuf.at[:, rows16(a), :], lrecv.at[a], 0)
        @pl.when(core != part)
        def _():
            r = part * 4 + zz
            send(KL, lbuf.at[:, rows16(r), :], lrecv.at[a], 0, dev_a(r))
    seven = pl.ds(0, 7)
    sent(KS, sb.at[seven])
    sent(KG, gb.at[seven])
    sent(KT, gtb.at[seven])
    sent(KQ, qb.at[seven, half[0]])
    sent(KH, qb.at[seven, half[1]])

    ysum[...] = jnp.zeros((4, 16, N), F32)
    arrived(KU, trecv, 0)
    tops = [trecv[r].astype(F32) for r in range(8)]
    tpair = [tops[2 * j] + tops[2 * j + 1] for j in range(4)]
    tquad = [tpair[0] + tpair[1], tpair[2] + tpair[3]]
    bsend[0] = tquad[0] + tquad[1]
    for r in range(7, 0, -1):
        @pl.when(r > y)
        def _():
            send(KB, bsend.at[0], brecv.at[y], y, dev_y(r))
    none = jnp.zeros((16, N), BF16)
    for r in range(8):
        vsend[r, 0] = tops[r - 1].astype(BF16) if r & 1 else none
        vsend[r, 1] = tpair[(r >> 1) ^ 1].astype(BF16) if r & 2 else none
        vsend[r, 2] = tquad[0].astype(BF16) if r & 4 else none
    mine = rows16(a)
    three = pl.ds(0, 3)
    for r in far:
        send(KV, vsend.at[r], rbuf.at[three, mine, :], 0, dev_a(r))
    local(KV, vsend.at[a], rbuf.at[three, mine, :], 0)
    sent(KU, trecv.at[seven])

    low = {}
    for r in range(1, 8):
        qt = qb[r].astype(F32)
        rows = gtb[r]
        for l in range(3):
            if r >> l & 1:
                part = nn((qt * rows[l : l + 1, :]).astype(BF16), gb[r])
                key = (l, r >> l)
                low[key] = low[key] + part if key in low else part
    for b in range(8):
        acc = jnp.zeros((N, N), F32)
        for l in range(3):
            if not b >> l & 1:
                acc = acc + low[(l, (b >> l) ^ 1)]
        dacc[b] = acc
    pair = [sb[2 * j].astype(F32) + sb[2 * j + 1].astype(F32) for j in range(4)]
    for b in range(8):
        acc = jnp.zeros((N, N), F32)
        rows = gtb[b]
        for l in range(3):
            if b >> l & 1:
                other = (b >> l) ^ 1
                if l == 0:
                    left = sb[other]
                elif l == 1:
                    left = pair[other].astype(BF16)
                else:
                    left = (pair[0] + pair[1]).astype(BF16)
                acc = acc + rows[l : l + 1, :] * nt(left, gb[b])
        ctr[b] = acc

    for r in range(7):
        @pl.when(r < y)
        def _():
            arrived(KB, brecv.at[r], r)
            high = jnp.where(y // 4 != r // 4, 2, jnp.where(y // 2 != r // 2, 1, 0))
            ysum[high] += brecv[r]
    for l in range(3):
        xsend[l] = ysum[l].astype(BF16)
    for r in far:
        send(KX, xsend, rbuf.at[pl.ds(3, 3), mine, :], 0, dev_a(r))
    local(KX, xsend, rbuf.at[pl.ds(3, 3), mine, :], 0)

    arrived(KL, lrecv, 0)
    for l in range(6, 9):
        total = lrecv[0, l - 3].astype(F32)
        for r in range(1, 8):
            total = total + lrecv[r, l - 3].astype(F32)
        bsend[l - 5] = total
    for r in range(7):
        @pl.when(r < y)
        def _():
            high = jnp.where(y // 4 != r // 4, 3, jnp.where(y // 2 != r // 2, 2, 1))
            send(KB, bsend.at[high], brecv.at[y], y, dev_y(r))
    lows = {}
    for l in range(3, 6):
        for r in range(8):
            if r >> (l - 3) & 1:
                lows[l, r] = lrecv[r, l - 3].astype(F32)
    sent(KL, lrecv.at[seven])
    sent(KV, vsend.at[seven])
    l4 = {3: lows[4, 2] + lows[4, 3], 7: lows[4, 6] + lows[4, 7]}
    l5 = (lows[5, 4] + lows[5, 5]) + (lows[5, 6] + lows[5, 7])
    dmid = []
    for r in range(8):
        acc = zero
        if not r & 1:
            acc = acc + lows[3, r + 1]
        if not r & 2:
            acc = acc + l4[r | 3]
        if not r & 4:
            acc = acc + l5
        dmid.append(acc)

    arrived(KV, rbuf.at[three], 0)

    def middle(b, _):
        rows = gtb[b]
        prod = nt(rbuf[0:3].reshape(3 * N, N), gb[b])
        acc = ctr[b]
        for l in range(3):
            acc = acc + rows[3 + l : 4 + l, :] * prod[l * N : (l + 1) * N]
        ctr[b] = acc
        return 0

    lax.fori_loop(0, 8, middle, 0, unroll=2)

    for r in range(1, 8):
        @pl.when(r > y)
        def _():
            arrived(KB, brecv.at[r], r)
            ysum[3] += brecv[r]
    dtop = ysum[3]
    for r in range(8):
        wsend[r] = (dmid[r] + dtop).astype(BF16)
    for r in far:
        send(KW, wsend.at[r], rbuf.at[6, mine, :], 0, dev_a(r))
    local(KW, wsend.at[a], rbuf.at[6, mine, :], 0)
    sent(KB, brecv.at[seven])
    sent(KX, rbuf.at[pl.ds(0, 3), pl.ds(0, 112), :])

    arrived(KX, rbuf.at[pl.ds(3, 3)], 0)
    for i, b in enumerate(near + [p]):
        rows = gtb[b]
        prod = nt(rbuf[3:6].reshape(3 * N, N), gb[b])
        acc = ctr[b]
        for l in range(3):
            acc = acc + rows[6 + l : 7 + l, :] * prod[l * N : (l + 1) * N]
        csend[b] = acc.T.astype(BF16)
        if i < 7:
            send(KC, csend.at[b], crecv.at[p], p, dev_p(b))
    local(KC, csend.at[p], crecv.at[p], p)

    sent(KW, wsend.at[seven])
    arrived(KW, rbuf.at[6], 0)
    dall = rbuf[6].astype(F32)
    for r in near:
        dsend[r] = (dacc[r] + dall).astype(BF16)
        send(KD, dsend.at[r], drecv.at[p], p, dev_p(r))
    dsend[p] = (dacc[p] + dall).astype(BF16)
    local(KD, dsend.at[p], drecv.at[p], p)

    for r in [p] + near:
        c = pl.ds(pl.multiple_of(r * N, N), N)
        arrived(KC, crecv.at[r], r)
        qo_ref[:, c] = (qloc[:, c] + crecv[r].astype(F32)).astype(BF16)
    sent(KC, csend.at[seven])
    for r in [p] + near:
        c = pl.ds(pl.multiple_of(r * N, N), N)
        arrived(KD, drecv.at[r], r)
        d = drecv[r]
        ko_ref[:, c] = (kloc[:, c] + nt(v_ref[:, c], d)).astype(BF16)
        vo_ref[:, c] = (vloc[:, c] + nn(k_ref[:, c], d)).astype(BF16)

    sent(KD, dsend.at[seven])


def write_out(qi, ki, vi, qo, ko, vo, sem):
    copies = [pltpu.make_async_copy(s, d, sem.at[i]) for i, (s, d) in enumerate(((qi, qo), (ki, ko), (vi, vo)))]
    for copy in copies:
        copy.start()
    for copy in copies:
        copy.wait()


def per_device(query_rows, key_rows, value_rows, out_grad, gate_class, gate_table):
    table = gate_table.transpose(1, 2, 0)
    out = jax.ShapeDtypeStruct((N, HEADS * N), BF16)
    vmem = pl.BlockSpec(memory_space=pltpu.VMEM)
    hbm = pl.BlockSpec(memory_space=pltpu.HBM)
    cube = lambda n, dtype: pltpu.VMEM((n, N, N), dtype)
    wide = pltpu.VMEM((N, HEADS * N), F32)
    flat = pltpu.VMEM((N, HEADS * N), BF16)
    outs = pl.pallas_call(
        kernel,
        out_shape=(out, out, out),
        in_specs=[hbm] * 6,
        out_specs=(vmem, vmem, vmem),
        scratch_shapes=[
            flat, flat, flat, flat,
            pltpu.VMEM((1, N), jnp.int32),
            pltpu.VMEM((20, HEADS, 32), F32),
            pltpu.VMEM((20 * HEADS, N), F32),
            pltpu.VMEM((HEADS, 24, N), F32),
            pltpu.VMEM((N, N), jnp.int32),
            cube(8, BF16), cube(8, BF16), cube(8, BF16), cube(8, BF16), cube(8, BF16),
            pltpu.VMEM((8, 16, N), F32),
            pltpu.VMEM((3 * N, N), F32),
            wide, wide, wide,
            pltpu.VMEM((N, N), BF16),
            cube(6, BF16),
            pltpu.VMEM((8, 16, N), BF16),
            pltpu.VMEM((8, 6, 16, N), BF16),
            pltpu.VMEM((4, 16, N), F32),
            pltpu.VMEM((8, 16, N), F32),
            pltpu.VMEM((4, 16, N), F32),
            pltpu.VMEM((8, 3, 16, N), BF16),
            pltpu.VMEM((8, 16, N), BF16),
            pltpu.VMEM((3, 16, N), BF16),
            cube(7, BF16),
            cube(8, F32), cube(8, F32),
            cube(8, BF16), cube(8, BF16), cube(8, BF16), cube(8, BF16),
            pltpu.SemaphoreType.DMA((6,)),
            pltpu.SemaphoreType.DMA((KINDS,)),
            pltpu.SemaphoreType.DMA((KINDS, 8)),
        ],
        compiler_params=pltpu.CompilerParams(
            collective_id=0, has_side_effects=True, vmem_limit_bytes=40 * 1024 * 1024
        ),
    )(*[pltpu.with_memory_space_constraint(one, pltpu.HBM) for one in (query_rows, key_rows, value_rows, out_grad, gate_class.reshape(1, N), table)])
    return pl.pallas_call(
        write_out,
        out_shape=(out, out, out),
        in_specs=[vmem] * 3,
        out_specs=(hbm, hbm, hbm),
        compiler_params=pltpu.CompilerParams(vmem_limit_bytes=16 * 1024 * 1024),
        scratch_shapes=[pltpu.SemaphoreType.DMA((3,))],
    )(*outs)


def solution(mesh):
    rows = P(("gx", "gy"), None)
    return jax.shard_map(
        per_device,
        mesh=mesh,
        in_specs=(rows, rows, rows, rows, P(("gx", "gy")), P()),
        out_specs=(rows, rows, rows),
        check_vma=False,
    )
```

```python
import jax
import jax.numpy as jnp
from jax import lax
from jax.experimental import pallas as pl
from jax.experimental.pallas import tpu as pltpu
from jax.sharding import PartitionSpec as P

MESH = pl.DeviceIdType.MESH
F32 = jnp.float32
BF16 = jnp.bfloat16
N = 128
HEADS = 8
KS, KG, KT, KQ, KH, KU, KL, KB, KV, KX, KW, KC, KD, KM = range(14)
KINDS = 14
NEAR = ((1, 2), (0, 2), (1, 1), (1, 3), (1, 0), (0, 1), (0, 3))
FAR = ((0, 2), (1, 2), (0, 1), (0, 3), (1, 1), (1, 3), (1, 0))


def mm(a, b, ca, cb):
    return lax.dot_general(a, b, (((ca,), (cb,)), ((), ())), preferred_element_type=F32)


def nn(a, b):
    return mm(a, b, 1, 0)


def nt(a, b):
    return mm(a, b, 1, 1)


def tn(a, b):
    return mm(a, b, 0, 0)


def kernel(
    q_hbm, k_hbm, v_hbm, g_hbm, cls_hbm, tab_hbm,
    qo_ref, ko_ref, vo_ref,
    q_ref, k_ref, v_ref, g_ref, cls_ref, tab_ref,
    gates, hg, lev_ref, st_send, qt_send, qb, gb, sb, gtb, lacc, qloc, kloc, vloc,
    tsend, lbuf, trecv, lrecv, bsend, brecv, ysum, vsend, wsend, xsend, rbuf, ctr, dacc, csend, dsend, crecv, drecv,
    lsem, ssem, rsem,
):
    gx = lax.axis_index("gx")
    gy = lax.axis_index("gy")
    y = gx // 2
    core = gx % 2
    zz = gy // 8
    p = gy % 8
    z0 = p // 4
    x = p % 4
    a = core * 4 + zz
    near = [(z0 + dz) % 2 * 4 + (x + dx) % 4 for dz, dx in NEAR]
    far = [(core + dc) % 2 * 4 + (zz + dz) % 4 for dc, dz in FAR]

    def dev_p(r):
        return (gx, zz * 8 + r)

    def dev_a(r):
        return (y * 2 + r // 4, (r % 4) * 8 + p)

    def dev_y(r):
        return (r * 2 + core, gy)

    barrier = pltpu.get_barrier_semaphore()
    for i, dy in enumerate((4, 3, 5, 2, 6, 1, 7)):
        for dev in (dev_a(far[i]), dev_y((y + dy) % 8), dev_p(near[i])):
            pl.semaphore_signal(barrier, inc=1, device_id=dev, device_id_type=MESH)

    loads = []
    for i, (src, dst) in enumerate((
        (cls_hbm, cls_ref), (tab_hbm, tab_ref), (q_hbm, q_ref), (g_hbm, g_ref), (k_hbm, k_ref), (v_hbm, v_ref),
    )):
        loads.append(pltpu.make_async_copy(src, dst, lsem.at[i]))
        loads[-1].start()

    def send(kind, src, dst, slot, dev):
        pltpu.make_async_remote_copy(
            src_ref=src, dst_ref=dst, send_sem=ssem.at[kind], recv_sem=rsem.at[kind, slot],
            device_id=dev, device_id_type=MESH,
        ).start()

    def sent(kind, like):
        pltpu.make_async_copy(like, like, ssem.at[kind]).wait()

    def local(kind, src, dst, slot):
        pltpu.make_async_copy(src, dst, rsem.at[kind, slot]).start()

    def arrived(kind, dst, slot):
        pltpu.make_async_copy(dst, dst, rsem.at[kind, slot]).wait()

    def cols(ref, r):
        return ref.at[:, pl.ds(pl.multiple_of(r * N, N), N)]

    def rows16(r):
        return pl.ds(pl.multiple_of(r * 16, 16), 16)

    zero = jnp.zeros((16, N), F32)
    loads[0].wait()
    loads[1].wait()
    classes = lax.broadcasted_iota(jnp.int32, (32, N), 0)
    onehot = (classes == cls_ref[...]).astype(F32)
    gates[...] = lax.dot_general(
        tab_ref[...].reshape(20 * HEADS, 32), onehot, (((1,), (0,)), ((), ())),
        precision=lax.Precision.HIGHEST, preferred_element_type=F32,
    )
    for h in range(HEADS):
        hg[h, 0:20] = gates[pl.ds(h, 20, stride=HEADS), :]
        hg[h, 20:24] = jnp.zeros((4, N), F32)
    loads[2].wait()
    loads[4].wait()
    loads[5].wait()
    for h in range(HEADS):
        c = slice(h * N, h * N + N)
        st_send[h] = tn(k_ref[:, c], v_ref[:, c]).astype(BF16)
        qt_send[h] = q_ref[:, c].T
    loads[3].wait()

    pl.semaphore_wait(barrier, 21)

    half = (pl.ds(0, 64), pl.ds(64, 64))
    for r in near:
        send(KS, st_send.at[r], sb.at[p], 0, dev_p(r))
    for r in near:
        send(KG, cols(g_ref, r), gb.at[p], p, dev_p(r))
        send(KT, hg.at[r, pl.ds(8, 16)], gtb.at[p], 0, dev_p(r))
    for r in near:
        send(KQ, qt_send.at[r, half[0]], qb.at[p, half[0]], p, dev_p(r))
    for r in near:
        send(KH, qt_send.at[r, half[1]], qb.at[p, half[1]], p, dev_p(r))
    local(KQ, qt_send.at[p, half[0]], qb.at[p, half[0]], p)
    local(KH, qt_send.at[p, half[1]], qb.at[p, half[1]], p)
    local(KS, st_send.at[p], sb.at[p], 0)
    local(KG, cols(g_ref, p), gb.at[p], p)
    local(KT, hg.at[p, pl.ds(8, 16)], gtb.at[p], 0)

    s_id = lax.broadcasted_iota(jnp.int32, (N, N), 0)
    t_id = lax.broadcasted_iota(jnp.int32, (N, N), 1)
    place = jnp.bitwise_xor(s_id, t_id)
    level = jnp.zeros((N, N), jnp.int32)
    for bit in range(7):
        level = level + (place >= 2**bit).astype(jnp.int32)
    lev_ref[...] = jnp.where(s_id <= t_id, level, -1)

    def own_head(h, _):
        c = pl.ds(pl.multiple_of(h * N, N), N)
        q = q_ref[:, c]
        k = k_ref[:, c]
        v = v_ref[:, c]
        g = g_ref[:, c]
        rows = hg[h, 0:8]
        lev = lev_ref[...]
        w = jnp.zeros((N, N), F32)
        for l in range(8):
            w = jnp.where(lev == l, rows[l : l + 1, :], w)
        wg = (w * nt(v, g)).astype(BF16)
        ws = (w * nt(k, q)).astype(BF16)
        kloc[:, c] = nn(wg, q)
        vloc[:, c] = nn(ws, g)
        qloc[:, c] = tn(wg, k)
        return 0

    lax.fori_loop(0, HEADS, own_head, 0)

    mine = rows16(a)
    three = pl.ds(0, 3)
    arrived(KS, sb, 0)
    states = [sb[r].astype(F32) for r in range(8)]
    pair = [states[2 * j] + states[2 * j + 1] for j in range(4)]
    tsend[...] = ((pair[0] + pair[1]) + (pair[2] + pair[3])).astype(BF16)
    for r in far:
        send(KU, tsend.at[rows16(r), :], trecv.at[a], 0, dev_a(r))
    local(KU, tsend.at[rows16(a), :], trecv.at[a], 0)

    arrived(KT, gtb, 0)
    def raise_half(part):
        for i, r in enumerate([p] + near):
            if part == 0:
                arrived(KG, gb.at[r], r)
            arrived((KQ, KH)[part], qb.at[r, half[part]], r)
            qt = qb[r, part * 64 : part * 64 + 64].astype(F32)
            rows = gtb[r]
            scaled = jnp.concatenate([(qt * rows[l : l + 1, :]).astype(BF16) for l in range(3, 9)], axis=0)
            prod = nn(scaled, gb[r])
            if i == 0:
                lacc[...] = prod
            elif i < 7:
                lacc[...] += prod
            else:
                lbuf[:, part * 64 : part * 64 + 64] = (lacc[...] + prod).astype(BF16).reshape(6, 64, N)
        for kind, levels in ((KL, pl.ds(3, 3)), (KM, pl.ds(0, 3))):
            for dz in (2, 1, 3):
                r = part * 4 + (zz + dz) % 4
                send(kind, lbuf.at[levels, rows16(r), :], lrecv.at[a, levels], 0, dev_a(r))
            @pl.when(core == part)
            def _():
                local(kind, lbuf.at[levels, rows16(a), :], lrecv.at[a, levels], 0)
            @pl.when(core != part)
            def _():
                r = part * 4 + zz
                send(kind, lbuf.at[levels, rows16(r), :], lrecv.at[a, levels], 0, dev_a(r))

    raise_half(0)
    raise_half(1)

    seven = pl.ds(0, 7)
    sent(KS, sb.at[seven])
    sent(KG, gb.at[seven])
    sent(KT, gtb.at[seven])
    sent(KQ, qb.at[seven, half[0]])
    sent(KH, qb.at[seven, half[1]])

    ysum[...] = jnp.zeros((4, 16, N), F32)
    arrived(KU, trecv, 0)
    tops = [trecv[r].astype(F32) for r in range(8)]
    tpair = [tops[2 * j] + tops[2 * j + 1] for j in range(4)]
    tquad = [tpair[0] + tpair[1], tpair[2] + tpair[3]]
    bsend[0] = tquad[0] + tquad[1]
    for r in range(7, 0, -1):
        @pl.when(r > y)
        def _():
            send(KB, bsend.at[0], brecv.at[y], y, dev_y(r))
    sent(KU, trecv.at[seven])

    low = {}
    for r in range(1, 8):
        qt = qb[r].astype(F32)
        rows = gtb[r]
        for l in range(3):
            if r >> l & 1:
                part = nn((qt * rows[l : l + 1, :]).astype(BF16), gb[r])
                key = (l, r >> l)
                low[key] = low[key] + part if key in low else part
    for b in range(8):
        acc = jnp.zeros((N, N), F32)
        for l in range(3):
            if not b >> l & 1:
                acc = acc + low[(l, (b >> l) ^ 1)]
        dacc[b] = acc
    pair = [sb[2 * j].astype(F32) + sb[2 * j + 1].astype(F32) for j in range(4)]
    for b in range(8):
        acc = jnp.zeros((N, N), F32)
        rows = gtb[b]
        for l in range(3):
            if b >> l & 1:
                other = (b >> l) ^ 1
                if l == 0:
                    left = sb[other]
                elif l == 1:
                    left = pair[other].astype(BF16)
                else:
                    left = (pair[0] + pair[1]).astype(BF16)
                acc = acc + rows[l : l + 1, :] * nt(left, gb[b])
        ctr[b] = acc

    arrived(KL, lrecv.at[:, pl.ds(3, 3)], 0)
    for l in range(6, 9):
        total = lrecv[0, l - 3].astype(F32)
        for r in range(1, 8):
            total = total + lrecv[r, l - 3].astype(F32)
        bsend[l - 5] = total
    for r in range(7):
        @pl.when(r < y)
        def _():
            high = jnp.where(y // 4 != r // 4, 3, jnp.where(y // 2 != r // 2, 2, 1))
            send(KB, bsend.at[high], brecv.at[y], y, dev_y(r))
    arrived(KM, lrecv.at[:, pl.ds(0, 3)], 0)
    lows = {}
    for l in range(3, 6):
        for r in range(8):
            if r >> (l - 3) & 1:
                lows[l, r] = lrecv[r, l - 3].astype(F32)
    sent(KL, lrecv.at[seven, pl.ds(0, 3)])
    sent(KM, lrecv.at[seven, pl.ds(0, 3)])
    l4 = {3: lows[4, 2] + lows[4, 3], 7: lows[4, 6] + lows[4, 7]}
    l5 = (lows[5, 4] + lows[5, 5]) + (lows[5, 6] + lows[5, 7])
    dmid = []
    for r in range(8):
        acc = zero
        if not r & 1:
            acc = acc + lows[3, r + 1]
        if not r & 2:
            acc = acc + l4[r | 3]
        if not r & 4:
            acc = acc + l5
        dmid.append(acc)

    none = jnp.zeros((16, N), BF16)
    for r in range(8):
        vsend[r, 0] = tops[r - 1].astype(BF16) if r & 1 else none
        vsend[r, 1] = tpair[(r >> 1) ^ 1].astype(BF16) if r & 2 else none
        vsend[r, 2] = tquad[0].astype(BF16) if r & 4 else none
    for r in far:
        send(KV, vsend.at[r], rbuf.at[three, mine, :], 0, dev_a(r))
    local(KV, vsend.at[a], rbuf.at[three, mine, :], 0)
    for r in range(7):
        @pl.when(r < y)
        def _():
            arrived(KB, brecv.at[r], r)
            high = jnp.where(y // 4 != r // 4, 2, jnp.where(y // 2 != r // 2, 1, 0))
            ysum[high] += brecv[r]
    for l in range(3):
        xsend[l] = ysum[l].astype(BF16)
    for r in far:
        send(KX, xsend, rbuf.at[pl.ds(3, 3), mine, :], 0, dev_a(r))
    local(KX, xsend, rbuf.at[pl.ds(3, 3), mine, :], 0)

    arrived(KV, rbuf.at[three], 0)

    def middle(b, _):
        rows = gtb[b]
        prod = nt(rbuf[0:3].reshape(3 * N, N), gb[b])
        acc = ctr[b]
        for l in range(3):
            acc = acc + rows[3 + l : 4 + l, :] * prod[l * N : (l + 1) * N]
        ctr[b] = acc
        return 0

    lax.fori_loop(0, 8, middle, 0, unroll=2)

    for r in range(1, 8):
        @pl.when(r > y)
        def _():
            arrived(KB, brecv.at[r], r)
            ysum[3] += brecv[r]
    dtop = ysum[3]
    for r in range(8):
        wsend[r] = (dmid[r] + dtop).astype(BF16)
    for r in far:
        send(KW, wsend.at[r], rbuf.at[6, mine, :], 0, dev_a(r))
    local(KW, wsend.at[a], rbuf.at[6, mine, :], 0)

    sent(KV, vsend.at[seven])
    sent(KB, brecv.at[seven])
    sent(KX, rbuf.at[pl.ds(0, 3), pl.ds(0, 112), :])
    arrived(KX, rbuf.at[pl.ds(3, 3)], 0)
    for i, b in enumerate(near + [p]):
        rows = gtb[b]
        prod = nt(rbuf[3:6].reshape(3 * N, N), gb[b])
        acc = ctr[b]
        for l in range(3):
            acc = acc + rows[6 + l : 7 + l, :] * prod[l * N : (l + 1) * N]
        csend[b] = acc.T.astype(BF16)
        if i < 7:
            send(KC, csend.at[b], crecv.at[p], p, dev_p(b))
    local(KC, csend.at[p], crecv.at[p], p)

    sent(KW, wsend.at[seven])
    arrived(KW, rbuf.at[6], 0)
    dall = rbuf[6].astype(F32)
    for r in near:
        dsend[r] = (dacc[r] + dall).astype(BF16)
        send(KD, dsend.at[r], drecv.at[p], p, dev_p(r))
    dsend[p] = (dacc[p] + dall).astype(BF16)
    local(KD, dsend.at[p], drecv.at[p], p)

    for r in [p] + near:
        c = pl.ds(pl.multiple_of(r * N, N), N)
        arrived(KC, crecv.at[r], r)
        qo_ref[:, c] = (qloc[:, c] + crecv[r].astype(F32)).astype(BF16)
    for r in [p] + near:
        c = pl.ds(pl.multiple_of(r * N, N), N)
        arrived(KD, drecv.at[r], r)
        d = drecv[r]
        ko_ref[:, c] = (kloc[:, c] + nt(v_ref[:, c], d)).astype(BF16)
        vo_ref[:, c] = (vloc[:, c] + nn(k_ref[:, c], d)).astype(BF16)

    sent(KC, csend.at[seven])
    sent(KD, dsend.at[seven])


def write_out(qi, ki, vi, qo, ko, vo, sem):
    copies = []
    for i, (src, dst) in enumerate(((qi, qo), (ki, ko), (vi, vo))):
        for j in range(2):
            rows = pl.ds(j * (N // 2), N // 2)
            copies.append(pltpu.make_async_copy(src.at[rows], dst.at[rows], sem.at[2 * i + j]))
    for copy in copies:
        copy.start()
    for copy in copies:
        copy.wait()


def per_device(query_rows, key_rows, value_rows, out_grad, gate_class, gate_table):
    table = gate_table.transpose(1, 2, 0)
    out = jax.ShapeDtypeStruct((N, HEADS * N), BF16)
    vmem = pl.BlockSpec(memory_space=pltpu.VMEM)
    hbm = pl.BlockSpec(memory_space=pltpu.HBM)
    cube = lambda n, dtype: pltpu.VMEM((n, N, N), dtype)
    wide = pltpu.VMEM((N, HEADS * N), F32)
    flat = pltpu.VMEM((N, HEADS * N), BF16)
    outs = pl.pallas_call(
        kernel,
        out_shape=(out, out, out),
        in_specs=[hbm] * 6,
        out_specs=(vmem, vmem, vmem),
        scratch_shapes=[
            flat, flat, flat, flat,
            pltpu.VMEM((1, N), jnp.int32),
            pltpu.VMEM((20, HEADS, 32), F32),
            pltpu.VMEM((20 * HEADS, N), F32),
            pltpu.VMEM((HEADS, 24, N), F32),
            pltpu.VMEM((N, N), jnp.int32),
            cube(8, BF16), cube(8, BF16), cube(8, BF16), cube(8, BF16), cube(8, BF16),
            pltpu.VMEM((8, 16, N), F32),
            pltpu.VMEM((3 * N, N), F32),
            wide, wide, wide,
            pltpu.VMEM((N, N), BF16),
            cube(6, BF16),
            pltpu.VMEM((8, 16, N), BF16),
            pltpu.VMEM((8, 6, 16, N), BF16),
            pltpu.VMEM((4, 16, N), F32),
            pltpu.VMEM((8, 16, N), F32),
            pltpu.VMEM((4, 16, N), F32),
            pltpu.VMEM((8, 3, 16, N), BF16),
            pltpu.VMEM((8, 16, N), BF16),
            pltpu.VMEM((3, 16, N), BF16),
            cube(7, BF16),
            cube(8, F32), cube(8, F32),
            cube(8, BF16), cube(8, BF16), cube(8, BF16), cube(8, BF16),
            pltpu.SemaphoreType.DMA((6,)),
            pltpu.SemaphoreType.DMA((KINDS,)),
            pltpu.SemaphoreType.DMA((KINDS, 8)),
        ],
        compiler_params=pltpu.CompilerParams(
            collective_id=0, has_side_effects=True, vmem_limit_bytes=40 * 1024 * 1024
        ),
    )(*[pltpu.with_memory_space_constraint(one, pltpu.HBM) for one in (query_rows, key_rows, value_rows, out_grad, gate_class.reshape(1, N), table)])
    return pl.pallas_call(
        write_out,
        out_shape=(out, out, out),
        in_specs=[vmem] * 3,
        out_specs=(hbm, hbm, hbm),
        compiler_params=pltpu.CompilerParams(vmem_limit_bytes=16 * 1024 * 1024),
        scratch_shapes=[pltpu.SemaphoreType.DMA((6,))],
    )(*outs)


def solution(mesh):
    rows = P(("gx", "gy"), None)
    return jax.shard_map(
        per_device,
        mesh=mesh,
        in_specs=(rows, rows, rows, rows, P(("gx", "gy")), P()),
        out_specs=(rows, rows, rows),
        check_vma=False,
    )
```

```python
import jax
import jax.numpy as jnp
from jax import lax
from jax.experimental import pallas as pl
from jax.experimental.pallas import tpu as pltpu
from jax.sharding import PartitionSpec as P

MESH = pl.DeviceIdType.MESH
F32 = jnp.float32
BF16 = jnp.bfloat16
N = 128
HEADS = 8
KS, KG, KT, KQ, KH, KU, KL, KB, KV, KX, KW, KC, KD, KM = range(14)
KINDS = 14
NEAR = ((1, 2), (0, 2), (1, 1), (1, 3), (1, 0), (0, 1), (0, 3))
FAR = ((0, 2), (1, 2), (0, 1), (0, 3), (1, 1), (1, 3), (1, 0))


def mm(a, b, ca, cb):
    return lax.dot_general(a, b, (((ca,), (cb,)), ((), ())), preferred_element_type=F32)


def nn(a, b):
    return mm(a, b, 1, 0)


def nt(a, b):
    return mm(a, b, 1, 1)


def tn(a, b):
    return mm(a, b, 0, 0)


def kernel(
    q_hbm, k_hbm, v_hbm, g_hbm, cls_hbm, tab_hbm,
    qo_ref, ko_ref, vo_ref,
    q_ref, k_ref, v_ref, g_ref, cls_ref, tab_ref,
    gates, hg, lev_ref, st_send, qt_send, qb, gb, sb, gtb, lacc, qloc, kloc, vloc,
    tsend, lbuf, trecv, lrecv, bsend, brecv, ysum, vsend, wsend, xsend, rbuf, ctr, dacc, csend, dsend, crecv, drecv,
    lsem, ssem, rsem,
):
    gx = lax.axis_index("gx")
    gy = lax.axis_index("gy")
    y = gx // 2
    core = gx % 2
    zz = gy // 8
    p = gy % 8
    z0 = p // 4
    x = p % 4
    a = core * 4 + zz
    near = [(z0 + dz) % 2 * 4 + (x + dx) % 4 for dz, dx in NEAR]
    far = [(core + dc) % 2 * 4 + (zz + dz) % 4 for dc, dz in FAR]

    def dev_p(r):
        return (gx, zz * 8 + r)

    def dev_a(r):
        return (y * 2 + r // 4, (r % 4) * 8 + p)

    def dev_y(r):
        return (r * 2 + core, gy)

    barrier = pltpu.get_barrier_semaphore()
    for i, dy in enumerate((4, 3, 5, 2, 6, 1, 7)):
        for dev in (dev_a(far[i]), dev_y((y + dy) % 8), dev_p(near[i])):
            pl.semaphore_signal(barrier, inc=1, device_id=dev, device_id_type=MESH)

    loads = []
    for i, (src, dst) in enumerate((
        (cls_hbm, cls_ref), (tab_hbm, tab_ref), (q_hbm, q_ref), (g_hbm, g_ref), (k_hbm, k_ref), (v_hbm, v_ref),
    )):
        loads.append(pltpu.make_async_copy(src, dst, lsem.at[i]))
        loads[-1].start()

    def send(kind, src, dst, slot, dev):
        pltpu.make_async_remote_copy(
            src_ref=src, dst_ref=dst, send_sem=ssem.at[kind], recv_sem=rsem.at[kind, slot],
            device_id=dev, device_id_type=MESH,
        ).start()

    def sent(kind, like):
        pltpu.make_async_copy(like, like, ssem.at[kind]).wait()

    def local(kind, src, dst, slot):
        pltpu.make_async_copy(src, dst, rsem.at[kind, slot]).start()

    def arrived(kind, dst, slot):
        pltpu.make_async_copy(dst, dst, rsem.at[kind, slot]).wait()

    def cols(ref, r):
        return ref.at[:, pl.ds(pl.multiple_of(r * N, N), N)]

    def rows16(r):
        return pl.ds(pl.multiple_of(r * 16, 16), 16)

    loads[3].wait()
    pl.semaphore_wait(barrier, 21)
    for r in near:
        send(KG, cols(g_ref, r), gb.at[p], p, dev_p(r))

    zero = jnp.zeros((16, N), F32)
    loads[0].wait()
    loads[1].wait()
    classes = lax.broadcasted_iota(jnp.int32, (32, N), 0)
    onehot = (classes == cls_ref[...]).astype(F32)
    gates[...] = lax.dot_general(
        tab_ref[...].reshape(20 * HEADS, 32), onehot, (((1,), (0,)), ((), ())),
        precision=lax.Precision.HIGHEST, preferred_element_type=F32,
    )
    for h in range(HEADS):
        hg[h, 0:20] = gates[pl.ds(h, 20, stride=HEADS), :]
        hg[h, 20:24] = jnp.zeros((4, N), F32)
    loads[2].wait()
    loads[4].wait()
    loads[5].wait()
    for h in range(HEADS):
        c = slice(h * N, h * N + N)
        st_send[h] = tn(k_ref[:, c], v_ref[:, c]).astype(BF16)
        qt_send[h] = q_ref[:, c].T

    half = (pl.ds(0, 64), pl.ds(64, 64))
    for r in near:
        send(KS, st_send.at[r], sb.at[p], 0, dev_p(r))
    for r in near:
        send(KT, hg.at[r, pl.ds(8, 16)], gtb.at[p], 0, dev_p(r))
    for r in near:
        send(KQ, qt_send.at[r, half[0]], qb.at[p, half[0]], p, dev_p(r))
    for r in near:
        send(KH, qt_send.at[r, half[1]], qb.at[p, half[1]], p, dev_p(r))
    local(KQ, qt_send.at[p, half[0]], qb.at[p, half[0]], p)
    local(KH, qt_send.at[p, half[1]], qb.at[p, half[1]], p)
    local(KS, st_send.at[p], sb.at[p], 0)
    local(KG, cols(g_ref, p), gb.at[p], p)
    local(KT, hg.at[p, pl.ds(8, 16)], gtb.at[p], 0)

    s_id = lax.broadcasted_iota(jnp.int32, (N, N), 0)
    t_id = lax.broadcasted_iota(jnp.int32, (N, N), 1)
    place = jnp.bitwise_xor(s_id, t_id)
    level = jnp.zeros((N, N), jnp.int32)
    for bit in range(7):
        level = level + (place >= 2**bit).astype(jnp.int32)
    lev_ref[...] = jnp.where(s_id <= t_id, level, -1)

    def own_head(h, _):
        c = pl.ds(pl.multiple_of(h * N, N), N)
        q = q_ref[:, c]
        k = k_ref[:, c]
        v = v_ref[:, c]
        g = g_ref[:, c]
        rows = hg[h, 0:8]
        lev = lev_ref[...]
        w = jnp.zeros((N, N), F32)
        for l in range(8):
            w = jnp.where(lev == l, rows[l : l + 1, :], w)
        wg = (w * nt(v, g)).astype(BF16)
        ws = (w * nt(k, q)).astype(BF16)
        kloc[:, c] = nn(wg, q)
        vloc[:, c] = nn(ws, g)
        qloc[:, c] = tn(wg, k)
        return 0

    lax.fori_loop(0, HEADS, own_head, 0)

    mine = rows16(a)
    three = pl.ds(0, 3)
    arrived(KS, sb, 0)
    states = [sb[r].astype(F32) for r in range(8)]
    pair = [states[2 * j] + states[2 * j + 1] for j in range(4)]
    tsend[...] = ((pair[0] + pair[1]) + (pair[2] + pair[3])).astype(BF16)
    for r in far:
        send(KU, tsend.at[rows16(r), :], trecv.at[a], 0, dev_a(r))
    local(KU, tsend.at[rows16(a), :], trecv.at[a], 0)

    arrived(KT, gtb, 0)
    def raise_half(part):
        for i, r in enumerate([p] + near):
            if part == 0:
                arrived(KG, gb.at[r], r)
            arrived((KQ, KH)[part], qb.at[r, half[part]], r)
            qt = qb[r, part * 64 : part * 64 + 64].astype(F32)
            rows = gtb[r]
            scaled = jnp.concatenate([(qt * rows[l : l + 1, :]).astype(BF16) for l in range(3, 9)], axis=0)
            prod = nn(scaled, gb[r])
            if i == 0:
                lacc[...] = prod
            elif i < 7:
                lacc[...] += prod
            else:
                lbuf[:, part * 64 : part * 64 + 64] = (lacc[...] + prod).astype(BF16).reshape(6, 64, N)
        for kind, levels in ((KL, pl.ds(3, 3)), (KM, pl.ds(0, 3))):
            for dz in (2, 1, 3):
                r = part * 4 + (zz + dz) % 4
                send(kind, lbuf.at[levels, rows16(r), :], lrecv.at[a, levels], 0, dev_a(r))
            @pl.when(core == part)
            def _():
                local(kind, lbuf.at[levels, rows16(a), :], lrecv.at[a, levels], 0)
            @pl.when(core != part)
            def _():
                r = part * 4 + zz
                send(kind, lbuf.at[levels, rows16(r), :], lrecv.at[a, levels], 0, dev_a(r))

    raise_half(0)
    raise_half(1)

    seven = pl.ds(0, 7)
    sent(KS, sb.at[seven])
    sent(KG, gb.at[seven])
    sent(KT, gtb.at[seven])
    sent(KQ, qb.at[seven, half[0]])
    sent(KH, qb.at[seven, half[1]])

    ysum[...] = jnp.zeros((4, 16, N), F32)
    arrived(KU, trecv, 0)
    tops = [trecv[r].astype(F32) for r in range(8)]
    tpair = [tops[2 * j] + tops[2 * j + 1] for j in range(4)]
    tquad = [tpair[0] + tpair[1], tpair[2] + tpair[3]]
    bsend[0] = tquad[0] + tquad[1]
    for r in range(7, 0, -1):
        @pl.when(r > y)
        def _():
            send(KB, bsend.at[0], brecv.at[y], y, dev_y(r))
    sent(KU, trecv.at[seven])

    low = {}
    for r in range(1, 8):
        qt = qb[r].astype(F32)
        rows = gtb[r]
        for l in range(3):
            if r >> l & 1:
                part = nn((qt * rows[l : l + 1, :]).astype(BF16), gb[r])
                key = (l, r >> l)
                low[key] = low[key] + part if key in low else part
    for b in range(8):
        acc = jnp.zeros((N, N), F32)
        for l in range(3):
            if not b >> l & 1:
                acc = acc + low[(l, (b >> l) ^ 1)]
        dacc[b] = acc
    pair = [sb[2 * j].astype(F32) + sb[2 * j + 1].astype(F32) for j in range(4)]
    for b in range(8):
        acc = jnp.zeros((N, N), F32)
        rows = gtb[b]
        for l in range(3):
            if b >> l & 1:
                other = (b >> l) ^ 1
                if l == 0:
                    left = sb[other]
                elif l == 1:
                    left = pair[other].astype(BF16)
                else:
                    left = (pair[0] + pair[1]).astype(BF16)
                acc = acc + rows[l : l + 1, :] * nt(left, gb[b])
        ctr[b] = acc

    arrived(KL, lrecv.at[:, pl.ds(3, 3)], 0)
    for l in range(6, 9):
        total = lrecv[0, l - 3].astype(F32)
        for r in range(1, 8):
            total = total + lrecv[r, l - 3].astype(F32)
        bsend[l - 5] = total
    for r in range(7):
        @pl.when(r < y)
        def _():
            high = jnp.where(y // 4 != r // 4, 3, jnp.where(y // 2 != r // 2, 2, 1))
            send(KB, bsend.at[high], brecv.at[y], y, dev_y(r))
    arrived(KM, lrecv.at[:, pl.ds(0, 3)], 0)
    lows = {}
    for l in range(3, 6):
        for r in range(8):
            if r >> (l - 3) & 1:
                lows[l, r] = lrecv[r, l - 3].astype(F32)
    sent(KL, lrecv.at[seven, pl.ds(0, 3)])
    sent(KM, lrecv.at[seven, pl.ds(0, 3)])
    l4 = {3: lows[4, 2] + lows[4, 3], 7: lows[4, 6] + lows[4, 7]}
    l5 = (lows[5, 4] + lows[5, 5]) + (lows[5, 6] + lows[5, 7])
    dmid = []
    for r in range(8):
        acc = zero
        if not r & 1:
            acc = acc + lows[3, r + 1]
        if not r & 2:
            acc = acc + l4[r | 3]
        if not r & 4:
            acc = acc + l5
        dmid.append(acc)

    none = jnp.zeros((16, N), BF16)
    for r in range(8):
        vsend[r, 0] = tops[r - 1].astype(BF16) if r & 1 else none
        vsend[r, 1] = tpair[(r >> 1) ^ 1].astype(BF16) if r & 2 else none
        vsend[r, 2] = tquad[0].astype(BF16) if r & 4 else none
    for r in far:
        send(KV, vsend.at[r], rbuf.at[three, mine, :], 0, dev_a(r))
    local(KV, vsend.at[a], rbuf.at[three, mine, :], 0)
    for r in range(7):
        @pl.when(r < y)
        def _():
            arrived(KB, brecv.at[r], r)
            high = jnp.where(y // 4 != r // 4, 2, jnp.where(y // 2 != r // 2, 1, 0))
            ysum[high] += brecv[r]
    for l in range(3):
        xsend[l] = ysum[l].astype(BF16)
    for r in far:
        send(KX, xsend, rbuf.at[pl.ds(3, 3), mine, :], 0, dev_a(r))
    local(KX, xsend, rbuf.at[pl.ds(3, 3), mine, :], 0)

    arrived(KV, rbuf.at[three], 0)

    def middle(b, _):
        rows = gtb[b]
        prod = nt(rbuf[0:3].reshape(3 * N, N), gb[b])
        acc = ctr[b]
        for l in range(3):
            acc = acc + rows[3 + l : 4 + l, :] * prod[l * N : (l + 1) * N]
        ctr[b] = acc
        return 0

    lax.fori_loop(0, 8, middle, 0, unroll=2)

    for r in range(1, 8):
        @pl.when(r > y)
        def _():
            arrived(KB, brecv.at[r], r)
            ysum[3] += brecv[r]
    dtop = ysum[3]
    for r in range(8):
        wsend[r] = (dmid[r] + dtop).astype(BF16)
    for r in far:
        send(KW, wsend.at[r], rbuf.at[6, mine, :], 0, dev_a(r))
    local(KW, wsend.at[a], rbuf.at[6, mine, :], 0)

    sent(KV, vsend.at[seven])
    sent(KB, brecv.at[seven])
    sent(KX, rbuf.at[pl.ds(0, 3), pl.ds(0, 112), :])
    arrived(KX, rbuf.at[pl.ds(3, 3)], 0)
    for i, b in enumerate(near + [p]):
        rows = gtb[b]
        prod = nt(rbuf[3:6].reshape(3 * N, N), gb[b])
        acc = ctr[b]
        for l in range(3):
            acc = acc + rows[6 + l : 7 + l, :] * prod[l * N : (l + 1) * N]
        csend[b] = acc.T.astype(BF16)
        if i < 7:
            send(KC, csend.at[b], crecv.at[p], p, dev_p(b))
    local(KC, csend.at[p], crecv.at[p], p)

    sent(KW, wsend.at[seven])
    arrived(KW, rbuf.at[6], 0)
    dall = rbuf[6].astype(F32)
    for r in near:
        dsend[r] = (dacc[r] + dall).astype(BF16)
        send(KD, dsend.at[r], drecv.at[p], p, dev_p(r))
    dsend[p] = (dacc[p] + dall).astype(BF16)
    local(KD, dsend.at[p], drecv.at[p], p)

    for r in [p] + near:
        c = pl.ds(pl.multiple_of(r * N, N), N)
        arrived(KC, crecv.at[r], r)
        qo_ref[:, c] = (qloc[:, c] + crecv[r].astype(F32)).astype(BF16)
    for r in [p] + near:
        c = pl.ds(pl.multiple_of(r * N, N), N)
        arrived(KD, drecv.at[r], r)
        d = drecv[r]
        ko_ref[:, c] = (kloc[:, c] + nt(v_ref[:, c], d)).astype(BF16)
        vo_ref[:, c] = (vloc[:, c] + nn(k_ref[:, c], d)).astype(BF16)

    sent(KC, csend.at[seven])
    sent(KD, dsend.at[seven])


def write_out(qi, ki, vi, qo, ko, vo, sem):
    copies = []
    for i, (src, dst) in enumerate(((qi, qo), (ki, ko), (vi, vo))):
        for j in range(2):
            rows = pl.ds(j * (N // 2), N // 2)
            copies.append(pltpu.make_async_copy(src.at[rows], dst.at[rows], sem.at[2 * i + j]))
    for copy in copies:
        copy.start()
    for copy in copies:
        copy.wait()


def per_device(query_rows, key_rows, value_rows, out_grad, gate_class, gate_table):
    table = gate_table.transpose(1, 2, 0)
    out = jax.ShapeDtypeStruct((N, HEADS * N), BF16)
    vmem = pl.BlockSpec(memory_space=pltpu.VMEM)
    hbm = pl.BlockSpec(memory_space=pltpu.HBM)
    cube = lambda n, dtype: pltpu.VMEM((n, N, N), dtype)
    wide = pltpu.VMEM((N, HEADS * N), F32)
    flat = pltpu.VMEM((N, HEADS * N), BF16)
    outs = pl.pallas_call(
        kernel,
        out_shape=(out, out, out),
        in_specs=[hbm] * 6,
        out_specs=(vmem, vmem, vmem),
        scratch_shapes=[
            flat, flat, flat, flat,
            pltpu.VMEM((1, N), jnp.int32),
            pltpu.VMEM((20, HEADS, 32), F32),
            pltpu.VMEM((20 * HEADS, N), F32),
            pltpu.VMEM((HEADS, 24, N), F32),
            pltpu.VMEM((N, N), jnp.int32),
            cube(8, BF16), cube(8, BF16), cube(8, BF16), cube(8, BF16), cube(8, BF16),
            pltpu.VMEM((8, 16, N), F32),
            pltpu.VMEM((3 * N, N), F32),
            wide, wide, wide,
            pltpu.VMEM((N, N), BF16),
            cube(6, BF16),
            pltpu.VMEM((8, 16, N), BF16),
            pltpu.VMEM((8, 6, 16, N), BF16),
            pltpu.VMEM((4, 16, N), F32),
            pltpu.VMEM((8, 16, N), F32),
            pltpu.VMEM((4, 16, N), F32),
            pltpu.VMEM((8, 3, 16, N), BF16),
            pltpu.VMEM((8, 16, N), BF16),
            pltpu.VMEM((3, 16, N), BF16),
            cube(7, BF16),
            cube(8, F32), cube(8, F32),
            cube(8, BF16), cube(8, BF16), cube(8, BF16), cube(8, BF16),
            pltpu.SemaphoreType.DMA((6,)),
            pltpu.SemaphoreType.DMA((KINDS,)),
            pltpu.SemaphoreType.DMA((KINDS, 8)),
        ],
        compiler_params=pltpu.CompilerParams(
            collective_id=0, has_side_effects=True, vmem_limit_bytes=40 * 1024 * 1024
        ),
    )(*[pltpu.with_memory_space_constraint(one, pltpu.HBM) for one in (query_rows, key_rows, value_rows, out_grad, gate_class.reshape(1, N), table)])
    return pl.pallas_call(
        write_out,
        out_shape=(out, out, out),
        in_specs=[vmem] * 3,
        out_specs=(hbm, hbm, hbm),
        compiler_params=pltpu.CompilerParams(vmem_limit_bytes=16 * 1024 * 1024),
        scratch_shapes=[pltpu.SemaphoreType.DMA((6,))],
    )(*outs)


def solution(mesh):
    rows = P(("gx", "gy"), None)
    return jax.shard_map(
        per_device,
        mesh=mesh,
        in_specs=(rows, rows, rows, rows, P(("gx", "gy")), P()),
        out_specs=(rows, rows, rows),
        check_vma=False,
    )
```
